32 devices in a mesh: tomo: 4 (over y, x), brick: 8 (over z, core).
Axes of the slice: x: 2, y: 2, z: 4, core: 2. Of those that a mesh axis runs over, the one named last changes fastest.
Arguments:
- features: bfloat16 [4, 64, 512, 128], P('tomo', 'brick'), may hold values from -6 to 6
- weight: bfloat16 [27, 128, 128], replicated, may hold values from -0.109375 to 0.109375
- cotangent: bfloat16 [4, 64, 512, 128], P('tomo', 'brick'), may hold values from -6 to 6
- brick_pos: int32 [4, 64], P('tomo', 'brick'), may hold values from 0 to 7, as said below
- brick_count: int32 [4, 8], P('tomo', 'brick'), may hold values from 3 to 8, as said below
Outputs:
- output: bfloat16 [4, 64, 512, 128], P('tomo', 'brick')
- input_grad: bfloat16 [4, 64, 512, 128], P('tomo', 'brick')
- weight_grad: float32 [27, 128, 128], replicated
The draws below stay inside these ranges and needn't reach their ends.
Inputs may be any that keep to these rules, and one draw needn't show every extreme that they name: `brick_count`: in every crop some device has all 8 positions occupied. `brick_pos`: the 8 slots of one device hold each position 0 to 7 once: first the occupied positions in increasing order, then the empty ones in increasing order.
All inputs are finite; a program needn't handle non-finite values.
Results may differ from the reference program's by a relative error of at most 0.001.
Values may be sent and summed in bfloat16 or wider, within the bound.
A program may use at most 128 MiB of HBM per device.

```python
import math
import jax
import jax.numpy as jnp
from jax import lax

C = 128
BE = 8
CAP = 8
VOX = 512
SLOTS = 64
N_TOMO = 4
N_BRICK = 8


def brick_layout(key):
    key_first = jax.random.fold_in(key, 11)
    key_second = jax.random.fold_in(key, 12)
    key_full = jax.random.fold_in(key, 13)
    key_order = jax.random.fold_in(key, 14)
    factor_a = jax.random.randint(key_first, (N_TOMO, N_BRICK), 0, CAP)
    factor_b = jax.random.randint(key_second, (N_TOMO, N_BRICK), 0, CAP)
    counts = jnp.minimum(3 + (factor_a + factor_b) // 2, CAP)
    full_device = jax.random.randint(key_full, (N_TOMO, 1), 0, N_BRICK)
    counts = jnp.where(jnp.arange(N_BRICK, dtype=jnp.int32)[None, :] == full_device, CAP, counts)
    scores = jax.random.randint(key_order, (N_TOMO, N_BRICK, CAP), 0, 1 << 20) * CAP + jnp.arange(CAP, dtype=jnp.int32)
    ranking = jnp.argsort(scores, axis=-1)
    rank_of = jnp.argsort(ranking, axis=-1)
    occupied = rank_of < counts[..., None]
    slot_keys = jnp.where(occupied, 0, CAP) + jnp.arange(CAP, dtype=jnp.int32)
    positions = jnp.argsort(slot_keys, axis=-1)
    return (counts.astype(jnp.int32), positions.reshape(N_TOMO, N_BRICK * CAP).astype(jnp.int32))


def draw_brick_pos(key, part):
    counts, positions = brick_layout(key)
    return positions


def draw_brick_count(key, part):
    counts, positions = brick_layout(key)
    return counts


def block_scale(own_key, shape, shards, smallest, largest):
    gain = 1.0
    for position, shards_of in shards:
        heights = jax.random.uniform(jax.random.fold_in(jax.random.fold_in(own_key, 6), position), (shards_of,), jnp.float32, smallest / len(shards), largest / len(shards))
        gain = gain * jnp.repeat(jnp.exp(heights), shape[position] // shards_of).reshape((-1,) + (1,) * (len(shape) - 1 - position))
    return gain


def centred(rng, shape, spread, limit, pieces=(), kind=jnp.bfloat16):
    array = jax.random.normal(rng, shape, jnp.float32) * spread
    if len(pieces) > 0:
        array = block_scale(rng, shape, pieces, -0.22, 0.18) * array
    return jnp.clip(array, min=-limit, max=limit).astype(kind)


def setup_inputs(seed: int = 0) -> dict:
    key_of = jax.random.split(jax.random.key(seed), 6)
    features = centred(key_of[0], (N_TOMO, SLOTS, VOX, C), 1.0, 6.0, ((0, 4), (1, 8)))
    weight = centred(key_of[1], (27, C, C), (27 * C) ** -0.5, 0.109375)
    cotangent = centred(key_of[2], (N_TOMO, SLOTS, VOX, C), 1.0, 6.0, ((0, 4), (1, 8)))
    brick_pos = draw_brick_pos(jax.random.fold_in(key_of[5], 71), 0)
    brick_count = draw_brick_count(jax.random.fold_in(key_of[5], 71), 0)
    return dict(features=features, weight=weight, cotangent=cotangent, brick_pos=brick_pos, brick_count=brick_count)


OFFSETS = [(shift_x, shift_y, shift_z) for shift_x in (-1, 0, 1) for shift_y in (-1, 0, 1) for shift_z in (-1, 0, 1)]

def cube_coords(index, levels):
    cube_x = jnp.zeros_like(index)
    cube_y = jnp.zeros_like(index)
    cube_z = jnp.zeros_like(index)
    for level in range(levels):
        cube_x = cube_x + ((index >> 3 * level + 2 & 1) << level)
        cube_y = cube_y + ((index >> 3 * level + 1 & 1) << level)
        cube_z = cube_z + ((index >> 3 * level & 1) << level)
    return (cube_x, cube_y, cube_z)

def tap_rows(window_x, extent, shift_x, shift_y, shift_z):
    channels = window_x.shape[-1]
    window_part = lax.slice(window_x, (1 + shift_x, 1 + shift_y, 1 + shift_z, 0), (1 + shift_x + extent, 1 + shift_y + extent, 1 + shift_z + extent, channels))
    return window_part.reshape(extent * extent * extent, channels)

def reference(features, weight, cotangent, brick_pos, brick_count):
    cube_side = 1
    levels = 0
    for level in range(12):
        if cube_side * cube_side * cube_side < N_BRICK:
            cube_side = cube_side * 2
            levels = levels + 1
    bricks_side = 2 * cube_side
    grid_span = BE * bricks_side
    slot_total = N_BRICK * CAP
    slot_ids = jnp.arange(slot_total, dtype=jnp.int32)
    device = slot_ids // CAP
    local_slot = slot_ids % CAP
    cube_x, cube_y, cube_z = cube_coords(device, levels)
    brick_shape = (BE, BE, BE, C)
    window_box = (BE + 2, BE + 2, BE + 2, C)

    def dense_grid(slots, brick_x, brick_y, brick_z):
        bricks = jnp.zeros((bricks_side, bricks_side, bricks_side) + brick_shape, slots.dtype)
        bricks = bricks.at[brick_x, brick_y, brick_z].set(slots.reshape((slot_total,) + brick_shape), mode='drop')
        grid = bricks.transpose(0, 3, 1, 4, 2, 5, 6).reshape(grid_span, grid_span, grid_span, C)
        return jnp.pad(grid, ((1, 1), (1, 1), (1, 1), (0, 0)))

    def per_crop(crop_args):
        slots_x, slots_g, positions, counts = crop_args
        active = local_slot < counts[device]
        brick_x = 2 * cube_x + (positions >> 2 & 1)
        brick_y = 2 * cube_y + (positions >> 1 & 1)
        brick_z = 2 * cube_z + (positions & 1)
        dropped_x = jnp.where(active, brick_x, bricks_side)
        padded_x = dense_grid(slots_x, dropped_x, brick_y, brick_z)
        padded_g = dense_grid(slots_g, dropped_x, brick_y, brick_z)

        def per_slot(weight_acc, index):
            corner = (BE * brick_x[index], BE * brick_y[index], BE * brick_z[index], jnp.int32(0))
            window_x = lax.dynamic_slice(padded_x, corner, window_box)
            window_g = lax.dynamic_slice(padded_g, corner, window_box)
            keep = active[index]
            grad_rows = jnp.where(keep, slots_g[index], jnp.zeros_like(slots_g[index]))
            summed_y = jnp.zeros((BE * BE * BE, C), jnp.float32)
            summed_dx = jnp.zeros((BE * BE * BE, C), jnp.float32)
            kernel_terms = []
            for k, (shift_x, shift_y, shift_z) in enumerate(OFFSETS):
                rows_x = tap_rows(window_x, BE, shift_x, shift_y, shift_z)
                rows_g = tap_rows(window_g, BE, -shift_x, -shift_y, -shift_z)
                summed_y = summed_y + jnp.dot(rows_x, weight[k], preferred_element_type=jnp.float32)
                summed_dx = summed_dx + jnp.dot(rows_g, weight[k].T, preferred_element_type=jnp.float32)
                kernel_terms.append(lax.dot_general(rows_x, grad_rows, (((0,), (0,)), ((), ())), preferred_element_type=jnp.float32))
            weight_acc = weight_acc + jnp.stack(kernel_terms)
            out_y = jnp.where(keep, summed_y, jnp.zeros_like(summed_y)).astype(jnp.bfloat16)
            out_dx = jnp.where(keep, summed_dx, jnp.zeros_like(summed_dx)).astype(jnp.bfloat16)
            return (weight_acc, (out_y, out_dx))
        weight_acc, (out_y, out_dx) = lax.scan(per_slot, jnp.zeros((27, C, C), jnp.float32), slot_ids)
        return (out_y, out_dx, weight_acc)
    out_y, out_dx, accs = lax.map(per_crop, (features, cotangent, brick_pos, brick_count))
    factor = 1.0 / math.sqrt(N_TOMO * N_BRICK * CAP * BE * BE * BE)
    weight_grad = lax.optimization_barrier(jnp.sum(accs, axis=0)) * factor
    return (out_y, out_dx, weight_grad)
```

```python
import functools
import math

import jax
import jax.numpy as jnp
from jax import lax
from jax.experimental import pallas as pl
from jax.experimental.pallas import tpu as pltpu
from jax.sharding import PartitionSpec as P

BE = 8
MESH = pl.DeviceIdType.MESH
TILE = 16
LEVELS = 32000.0


def coords_of(index, levels):
    out = []
    for bit in (2, 1, 0):
        c = 0
        for level in range(levels):
            c = c + lax.rem(index // (1 << (3 * level + bit)), 2) * (1 << level)
        out.append(c)
    return out


def index_of(coords, levels):
    i = 0
    for bit, c in zip((2, 1, 0), coords):
        for level in range(levels):
            i = i + lax.rem(c // (1 << level), 2) * (1 << (3 * level + bit))
    return i


def kernel(
    factor, tb, bb, groups,
    pos_ref, cnt_ref, f_ref, g_ref, w_ref,
    out_ref, dx_ref, dw_ref,
    pad, zs, zr, wx, gt, obuf, src, land, tot, own, qs, ql, fs, fl, aq, cq,
    hsend, hrecv, csend, crecv, rsend, rrecv, fsend, frecv, gsend, grecv,
):
    e = 2 * BE
    half = e // 2
    ch = f_ref.shape[-1]
    tap = ch // TILE
    levels = bb // 3
    side = 1 << levels
    tomo = lax.axis_index("tomo")
    brick = lax.axis_index("brick")
    here = coords_of(brick, levels)

    near = []
    for axis in range(3):
        above, below = list(here), list(here)
        above[axis] = here[axis] + 1
        below[axis] = here[axis] + side - 1
        near.append((
            here[axis] < side - 1, (tomo, index_of(above, levels)),
            here[axis] > 0, (tomo, index_of(below, levels)),
        ))

    def mate_on(v, width):
        bit = lax.rem(v // width, 2)
        return bit, v + width - 2 * width * bit

    core_bit, core_mate = mate_on(brick, 1)
    core = (tomo, core_mate)
    flips = [(0, 1 << k) for k in range(tb)] + [(1, 2)]
    blk = 1 << len(flips)
    home = 0
    for k, (axis, width) in enumerate(flips):
        home = home + lax.rem((tomo, brick)[axis] // width, 2) * (1 << k)
    peers = []
    for r in range(blk):
        at, rank = [tomo, brick], home
        for k, (axis, width) in enumerate(flips):
            if r >> k & 1:
                at[axis] = mate_on(at[axis], width)[1]
                rank = mate_on(rank, 1 << k)[1]
        peers.append((rank, tuple(at)))
    far = []
    for k in range(2, bb):
        bit, mate = mate_on(brick, 1 << k)
        far.append((bit, (tomo, mate)))

    barrier = pltpu.get_barrier_semaphore()
    greet = [core] + [mate for _, mate in peers[1:]] + [mate for _, mate in far]
    count = len(greet)
    for mate in greet:
        pl.semaphore_signal(barrier, inc=1, device_id=mate, device_id_type=MESH)
    for has_above, above, has_below, below in near:
        for has, mate in ((has_above, above), (has_below, below)):

            @pl.when(has)
            def _(mate=mate):
                pl.semaphore_signal(barrier, inc=1, device_id=mate, device_id_type=MESH)

            count = count + has.astype(jnp.int32)

    slots = []
    for p in range(8):
        s = jnp.int32(0)
        for k in range(8):
            s = jnp.where(pos_ref[k] == p, k, s)
        slots.append(s)

    def gather(x, carry):
        for a, ref in ((0, f_ref), (1, g_ref)):
            for q in range(4):
                parts = []
                for pz in range(2):
                    s = slots[2 * q + pz]
                    v = ref[s, x].astype(jnp.float32)
                    parts.append(jnp.where(s < cnt_ref[0], v, 0.0))
                pad[a, 1, 1 + q // 2 * BE + x, pl.ds(1 + q % 2 * BE, BE)] = jnp.concatenate(
                    parts, axis=1
                ).astype(pad.dtype)
        return carry

    lax.fori_loop(0, BE, gather, 0)
    pl.semaphore_wait(barrier, count)

    def face(axis, a, at):
        if axis == 0:
            return pad.at[a, 1, at, pl.ds(1, e)]
        return pad.at[a, 1, :, at]

    def ends(axis, a):
        if axis == 2:
            return (zs.at[0, a], zr.at[0, a]), (zs.at[1, a], zr.at[1, a])
        return (face(axis, a, e), face(axis, a, 0)), (face(axis, a, 1), face(axis, a, e + 1))

    def halo_copies(axis, a):
        has_above, above, has_below, below = near[axis]
        up, down = ends(axis, a)
        made = []
        for k, (ends_k, mate) in enumerate(((up, above), (down, below))):
            made.append(pltpu.make_async_remote_copy(
                src_ref=ends_k[0], dst_ref=ends_k[1],
                send_sem=hsend.at[axis, a, k], recv_sem=hrecv.at[axis, a, k],
                device_id=mate, device_id_type=MESH,
            ))
        return made, (has_above, has_below)

    def halo_start(axis, a):
        made, has = halo_copies(axis, a)
        for k in range(2):

            @pl.when(has[k])
            def _(k=k):
                made[k].start()

    def halo_finish(axis, a):
        made, has = halo_copies(axis, a)
        for k in range(2):

            @pl.when(has[1 - k])
            def _(k=k):
                made[k].wait_recv()

            @pl.when(jnp.logical_not(has[1 - k]))
            def _(k=k):
                if axis == 0:
                    pad[a, 1, (0, e + 1)[k], pl.ds(1, e)] = jnp.zeros((e, e, ch), pad.dtype)
                elif axis == 1:
                    pad[a, 1, :, (0, e + 1)[k]] = jnp.zeros((e + 2, e, ch), pad.dtype)
                else:
                    zr[k, a] = jnp.zeros((e + 2, e + 2, ch), zr.dtype)

            @pl.when(has[k])
            def _(k=k):
                made[k].wait_send()

    halo_start(0, 0)
    halo_start(0, 1)

    zero = jnp.zeros((ch, ch), wx.dtype)

    def spread(t, carry):
        ox, oz = t // 3, lax.rem(t, 3)
        for i in range(4):
            for p in range(2):
                oy = i - p
                at = (pl.ds(i * ch, ch), pl.ds(p * ch, ch))
                if 0 <= oy <= 2:
                    wx[(0, t) + at] = w_ref[ox * 9 + oy * 3 + oz]
                    wx[(1, t) + at] = w_ref[(2 - ox) * 9 + (2 - oy) * 3 + 2 - oz].T
                else:
                    wx[(0, t) + at] = zero
                    wx[(1, t) + at] = zero
        return carry

    lax.fori_loop(0, 9, spread, 0)
    halo_finish(0, 0)
    halo_start(1, 0)

    def turn(c, carry):
        for x in range(2):
            own = pad[1, 1, 2 * c + x + 1, pl.ds(1, e)].reshape(half, 2, e, ch)
            for p in range(2):
                gt[c, pl.ds(p * ch, ch), pl.ds(x * half * e, half * e)] = (
                    own[:, p].reshape(half * e, ch).T
                )
        return carry

    lax.fori_loop(0, half, turn, 0)
    halo_finish(1, 0)

    def edges(a):
        def body(x, carry):
            v = pad[a, 1, x].astype(jnp.float32)
            zs[0, a, x] = v[:, e - 1]
            zs[1, a, x] = v[:, 0]
            return carry

        lax.fori_loop(0, e + 2, body, 0)

    edges(0)
    halo_start(2, 0)
    halo_finish(0, 1)
    halo_start(1, 1)
    halo_finish(2, 0)

    zidx = lax.broadcasted_iota(jnp.int32, (1, e, 1), 1)

    def shift(a):
        def body(x, carry):
            mid = pad[a, 1, x].astype(jnp.float32)
            lo = zr[0, a, x][:, None, :]
            hi = zr[1, a, x][:, None, :]
            pad[a, 0, x] = jnp.where(zidx == 0, lo, pltpu.roll(mid, 1, 1)).astype(pad.dtype)
            pad[a, 2, x] = jnp.where(zidx == e - 1, hi, pltpu.roll(mid, e - 1, 1)).astype(pad.dtype)
            return carry

        lax.fori_loop(0, e + 2, body, 0)

    def rows(a, oz, x0, nx):
        v = pad[a, oz, pl.ds(x0, nx)].reshape(nx, half + 1, 2, e, ch)
        parts = [
            v[:, i // 2:i // 2 + half, i % 2].reshape(nx * half * e, ch) for i in range(4)
        ]
        return jnp.concatenate(parts, axis=1)

    def terms(t, carry):
        ox, oz = t // 3, lax.rem(t, 3)
        acc = jnp.zeros((2 * ch, 4 * ch), jnp.float32)
        for c in range(half):
            acc = acc + jnp.dot(
                gt[c], rows(0, oz, ox + 2 * c, 2), preferred_element_type=jnp.float32
            )
        for oy in range(3):
            block = acc[:ch, oy * ch:(oy + 1) * ch] + acc[ch:, (oy + 1) * ch:(oy + 2) * ch]
            src[pl.ds((t * 3 + oy) * tap, tap)] = block.T.reshape(tap, TILE, ch)
        return carry

    def to_mate(source, target, send, recv, mate):
        return pltpu.make_async_remote_copy(
            src_ref=source, dst_ref=target, send_sem=send, recv_sem=recv,
            device_id=mate, device_id_type=MESH,
        )

    def parts(s):
        base, size = groups[s]
        return base, size // 2, size // 2 // blk

    def core_copy(s):
        base, half_size, _ = parts(s)
        return to_mate(
            src.at[pl.ds(base + (1 - core_bit) * half_size, half_size)],
            land.at[pl.ds(base // 2, half_size)], csend.at[0, s], crecv.at[0, s], core,
        )

    def block_copy(s, r):
        size = pl.ds(0, parts(s)[2] + 1)
        return to_mate(
            qs.at[s, r, size], ql.at[s, r, size], rsend.at[s, r], rrecv.at[s, r], peers[r][1]
        )

    def far_copy(s, k):
        size = pl.ds(0, parts(s)[2] + 1)
        return to_mate(fs.at[s, k, size], fl.at[s, k, size], fsend.at[s, k], frecv.at[s, k], far[k][1])

    def gather_copy(s, r):
        size = pl.ds(0, parts(s)[2] + 1)
        return to_mate(
            aq.at[s, 0, size], aq.at[s, r, size], gsend.at[s, r], grecv.at[s, r], peers[r][1]
        )

    def back_copy(s):
        return to_mate(aq.at[s], cq.at[s], csend.at[1, s], crecv.at[1, s], core)

    def encode(v):
        top = jnp.max(jnp.abs(v), axis=0)
        power = jnp.clip(jnp.ceil(jnp.log2(top)), -126.0, 126.0)
        code = jnp.round(v * jnp.exp2(-power) * LEVELS)
        return code.astype(jnp.int32).astype(jnp.int16), power.astype(jnp.int32).astype(jnp.int16)

    def decode(code, power):
        scale = jnp.exp2(power.astype(jnp.int32).astype(jnp.float32))
        return code.astype(jnp.int32).astype(jnp.float32) * (1.0 / LEVELS) * scale

    def put_code(ref, size, v):
        code, power = encode(v)
        ref[pl.ds(0, size)] = code
        ref[size] = power

    def get_code(ref, size):
        return decode(ref[pl.ds(0, size)], ref[size])

    def begin(s):
        core_copy(s).start()

    def split(s):
        base, half_size, size = parts(s)
        core_copy(s).wait()
        order = sorted(range(1, blk), key=lambda r: -bin(r).count("1")) + [0]
        for r in order:
            at = peers[r][0] * size
            v = src[pl.ds(base + core_bit * half_size + at, size)] + land[pl.ds(base // 2 + at, size)]
            if r == 0:
                own[s, pl.ds(0, size)] = v
            else:
                put_code(qs.at[s, r], size, v)
                block_copy(s, r).start()

    def spread_out(s, v):
        put_code(aq.at[s, 0], parts(s)[2], v * factor)
        for r in sorted(range(1, blk), key=lambda r: -bin(r).count("1")):
            gather_copy(s, r).start()

    def join(s):
        size = parts(s)[2]
        v = own[s, pl.ds(0, size)]
        for r in range(1, blk):
            block_copy(s, r).wait()
            v = v + get_code(ql.at[s, r], size)
        if far:
            put_code(fs.at[s, 0], size, v)
            far_copy(s, 0).start()
        else:
            spread_out(s, v)

    def cross(s, k):
        size = parts(s)[2]
        far_copy(s, k).wait()
        mine, theirs = fs[s, k, pl.ds(0, size + 1)].astype(jnp.int32), fl[s, k, pl.ds(0, size + 1)].astype(jnp.int32)
        low = jnp.where(far[k][0] == 0, mine, theirs)
        high = jnp.where(far[k][0] == 0, theirs, mine)
        v = decode(low[:size], low[size]) + decode(high[:size], high[size])
        if k + 1 < len(far):
            put_code(fs.at[s, k + 1], size, v)
            far_copy(s, k + 1).start()
        else:
            spread_out(s, v)

    def relay(s):
        for r in range(1, blk):
            gather_copy(s, r).wait()
        back_copy(s).start()
        unpack(s, aq, core_bit, [peers[r][0] for r in range(blk)])

    def unpack(s, ref, bit, ranks):
        base, half_size, size = parts(s)
        for r in range(blk):
            tot[pl.ds(base + bit * half_size + ranks[r] * size, size)] = get_code(ref.at[s, r], size)

    def close(s):
        back_copy(s).wait()
        unpack(s, cq, 1 - core_bit, [peers[r][0] for r in range(blk)])

    nx = 4

    def conv(a, c):
        x0 = c * nx
        acc = jnp.zeros((nx * half * e, 2 * ch), jnp.float32)
        for t in range(9):
            acc = acc + jnp.dot(
                rows(a, t % 3, x0 + t // 3, nx), wx[a, t], preferred_element_type=jnp.float32
            )
        for p in range(2):
            obuf[a, pl.ds(x0, nx), :, p] = (
                acc[:, p * ch:(p + 1) * ch].reshape(nx, half, 2, BE, ch).astype(obuf.dtype)
            )

    def put(a, dst):
        for s in range(8):
            p = pos_ref[s]
            v = obuf[
                a, pl.ds(p // 4 * BE, BE), pl.ds(lax.rem(p // 2, 2) * (BE // 2), BE // 2), :,
                lax.rem(p, 2),
            ].reshape(BE, BE, BE, ch)
            dst[s] = jnp.where(s < cnt_ref[0], v, jnp.zeros_like(v))

    work = []
    for a, dst in ((0, out_ref), (1, dx_ref)):
        if a == 1:
            work.append(functools.partial(halo_finish, 2, 1))
            work.append(functools.partial(shift, 1))
        for c in range(e // nx):
            work.append(functools.partial(conv, a, c))
        work.append(functools.partial(put, a, dst))

    shift(0)
    used = 27 * tap
    if src.shape[0] > used:
        src[pl.ds(used, src.shape[0] - used)] = jnp.zeros((src.shape[0] - used, TILE, ch), src.dtype)
    early = -(-groups[1][0] // (3 * tap))
    lax.fori_loop(0, early, terms, 0)
    begin(0)
    halo_finish(1, 1)
    edges(1)
    halo_start(2, 1)
    middle = min(early + 2, 9)
    lax.fori_loop(early, middle, terms, 0)
    split(0)
    lax.fori_loop(middle, 9, terms, 0)
    begin(1)

    def do(n):
        for _ in range(n):
            if work:
                work.pop(0)()

    do(1)
    split(1)
    do(4)
    join(0)
    do(3)
    join(1)
    do(2)
    steps = [functools.partial(cross, s, k) for k in range(len(far)) for s in range(2)]
    for step in steps[:1]:
        step()
    do(2)
    for step in steps[1:]:
        step()
    do(len(work))
    relay(0)
    close(0)
    relay(1)
    close(1)

    def lay(t, carry):
        for oy in range(3):
            dw_ref[t // 3 * 9 + oy * 3 + lax.rem(t, 3)] = tot[
                pl.ds((t * 3 + oy) * tap, tap)
            ].reshape(ch, ch)
        return carry

    lax.fori_loop(0, 9, lay, 0)


def fused(features, cotangent, weight, pos, cnt, factor, n_tomo, n_brick):
    slots, vox, ch = features.shape
    e = 2 * BE
    half = e // 2
    n = n_tomo * n_brick
    tb, bb = n_tomo.bit_length() - 1, n_brick.bit_length() - 1
    blk = 1 << (tb + 1)
    unit = 2 * blk
    units = -(-weight.shape[0] * (ch // TILE) // unit)
    first = units // 2
    groups = [(0, first * unit), (first * unit, (units - first) * unit)]
    total = units * unit
    piece = (units - first) + 1
    far = max(bb - 2, 1)
    vm = pl.BlockSpec(memory_space=pltpu.VMEM)
    sm = pl.BlockSpec(memory_space=pltpu.SMEM)
    brick = jax.ShapeDtypeStruct((slots, BE, BE, BE, ch), jnp.bfloat16)
    dma = pltpu.SemaphoreType.DMA
    return pl.pallas_call(
        functools.partial(kernel, factor, tb, bb, groups),
        out_shape=(brick, brick, jax.ShapeDtypeStruct(weight.shape, jnp.float32)),
        in_specs=[sm, sm, vm, vm, vm],
        out_specs=(vm, vm, vm),
        scratch_shapes=[
            pltpu.VMEM((2, 3, e + 2, e + 2, e, ch), jnp.bfloat16),
            pltpu.VMEM((2, 2, e + 2, e + 2, ch), jnp.float32),
            pltpu.VMEM((2, 2, e + 2, e + 2, ch), jnp.float32),
            pltpu.VMEM((2, 9, 4 * ch, 2 * ch), jnp.bfloat16),
            pltpu.VMEM((half, 2 * ch, 2 * half * e), jnp.bfloat16),
            pltpu.VMEM((2, e, half, 2, 2, BE, ch), jnp.bfloat16),
            pltpu.VMEM((total, TILE, ch), jnp.float32),
            pltpu.VMEM((total // 2, TILE, ch), jnp.float32),
            pltpu.VMEM((total, TILE, ch), jnp.float32),
            pltpu.VMEM((2, piece - 1, TILE, ch), jnp.float32),
            pltpu.VMEM((2, blk, piece, TILE, ch), jnp.int16),
            pltpu.VMEM((2, blk, piece, TILE, ch), jnp.int16),
            pltpu.VMEM((2, far, piece, TILE, ch), jnp.int16),
            pltpu.VMEM((2, far, piece, TILE, ch), jnp.int16),
            pltpu.VMEM((2, blk, piece, TILE, ch), jnp.int16),
            pltpu.VMEM((2, blk, piece, TILE, ch), jnp.int16),
            dma((3, 2, 2)), dma((3, 2, 2)), dma((2, 2)), dma((2, 2)),
            dma((2, blk)), dma((2, blk)), dma((2, far)), dma((2, far)), dma((2, blk)), dma((2, blk)),
        ],
        compiler_params=pltpu.CompilerParams(
            collective_id=0, has_side_effects=True, vmem_limit_bytes=58 << 20
        ),
        name="fused",
    )(
        pos, cnt,
        features.reshape(slots, BE, BE, BE, ch), cotangent.reshape(slots, BE, BE, BE, ch), weight,
    )


def shards(features, weight, cotangent, brick_pos, brick_count):
    slots, vox, ch = features.shape[1:]
    n_tomo, n_brick = lax.axis_size("tomo"), lax.axis_size("brick")
    factor = 1.0 / math.sqrt(n_tomo * n_brick * slots * vox)
    out, dx, dw = fused(
        features[0], cotangent[0], weight, brick_pos[0], brick_count[0], factor, n_tomo, n_brick
    )
    return out.reshape(1, slots, vox, ch), dx.reshape(1, slots, vox, ch), dw


def solution(mesh):
    in_specs = (
        P("tomo", "brick", None, None),
        P(),
        P("tomo", "brick", None, None),
        P("tomo", "brick"),
        P("tomo", "brick"),
    )
    out_specs = (P("tomo", "brick", None, None), P("tomo", "brick", None, None), P())
    return jax.shard_map(shards, mesh=mesh, in_specs=in_specs, out_specs=out_specs, check_vma=False)
```

```python
import functools
import math

import jax
import jax.numpy as jnp
from jax import lax
from jax.experimental import pallas as pl
from jax.experimental.pallas import tpu as pltpu
from jax.sharding import PartitionSpec as P

BE = 8
MESH = pl.DeviceIdType.MESH
TILE = 16
LEVELS = 32000.0


def coords_of(index, levels):
    out = []
    for bit in (2, 1, 0):
        c = 0
        for level in range(levels):
            c = c + lax.rem(index // (1 << (3 * level + bit)), 2) * (1 << level)
        out.append(c)
    return out


def index_of(coords, levels):
    i = 0
    for bit, c in zip((2, 1, 0), coords):
        for level in range(levels):
            i = i + lax.rem(c // (1 << level), 2) * (1 << (3 * level + bit))
    return i


def kernel(
    factor, tb, bb, groups,
    pos_hbm, cnt_hbm, f_hbm, g_hbm, w_hbm,
    out_ref, dx_ref, dw_ref,
    pos_ref, cnt_ref, f_ref, g_ref, w_ref, pad, zs, zr, wx, gt, obuf, src, land, own, qs, ql, fs, fl, aq, cq,
    isem, hsend, hrecv, psend, precv, csend, crecv, rsend, rrecv, fsend, frecv, gsend, grecv,
):
    e = 2 * BE
    half = e // 2
    ch = f_ref.shape[-1]
    tap = ch // TILE
    levels = bb // 3
    side = 1 << levels
    tomo = lax.axis_index("tomo")
    brick = lax.axis_index("brick")
    here = coords_of(brick, levels)

    loads = [
        pltpu.make_async_copy(source, target, isem.at[k])
        for k, (source, target) in enumerate((
            (pos_hbm, pos_ref), (cnt_hbm, cnt_ref), (f_hbm, f_ref), (g_hbm, g_ref), (w_hbm, w_ref)
        ))
    ]
    for load in loads:
        load.start()

    def neighbour(step):
        at, has = [], True
        for c, d in zip(here, step):
            at.append(lax.rem(c + d + side, side))
            if d:
                has = jnp.logical_and(has, c < side - 1 if d > 0 else c > 0)
        return has, (tomo, index_of(at, levels))

    flat = [(i, j, 0) for i in (-1, 0, 1) for j in (-1, 0, 1) if i or j]
    upright = [(0, 0, 1), (0, 0, -1)]
    near = {step: neighbour(step) for step in flat + upright}

    def mate_on(v, width):
        bit = lax.rem(v // width, 2)
        return bit, v + width - 2 * width * bit

    core_bit, core_mate = mate_on(brick, 1)
    core = (tomo, core_mate)
    flips = [(0, 1 << k) for k in range(tb)] + [(1, 2)]
    blk = 1 << len(flips)
    home = 0
    for k, (axis, width) in enumerate(flips):
        home = home + lax.rem((tomo, brick)[axis] // width, 2) * (1 << k)
    peers = []
    for r in range(blk):
        at, rank = [tomo, brick], home
        for k, (axis, width) in enumerate(flips):
            if r >> k & 1:
                at[axis] = mate_on(at[axis], width)[1]
                rank = mate_on(rank, 1 << k)[1]
        peers.append((rank, tuple(at)))
    far = []
    for k in range(2, bb):
        bit, mate = mate_on(brick, 1 << k)
        far.append((bit, (tomo, mate)))

    barrier = pltpu.get_barrier_semaphore()
    greet = [core] + [mate for _, mate in peers[1:]] + [mate for _, mate in far]
    count = len(greet)
    for mate in greet:
        pl.semaphore_signal(barrier, inc=1, device_id=mate, device_id_type=MESH)
    for has, mate in near.values():

        @pl.when(has)
        def _(mate=mate):
            pl.semaphore_signal(barrier, inc=1, device_id=mate, device_id_type=MESH)

        count = count + has.astype(jnp.int32)

    loads[0].wait()
    loads[1].wait()

    slots = []
    for p in range(8):
        s = jnp.int32(0)
        for k in range(8):
            s = jnp.where(pos_ref[0, k] == p, k, s)
        slots.append(s)

    def gather(a, ref):
        def body(x, carry):
            for q in range(4):
                parts = []
                for pz in range(2):
                    s = slots[2 * q + pz]
                    v = ref[s, x].astype(jnp.float32)
                    parts.append(jnp.where(s < cnt_ref[0, 0], v, 0.0))
                pad[a, 1, 1 + q // 2 * BE + x, pl.ds(1 + q % 2 * BE, BE)] = jnp.concatenate(
                    parts, axis=1
                ).astype(pad.dtype)
            return carry

        lax.fori_loop(0, BE, body, 0)

    def span(d, inner):
        if d == 0:
            return pl.ds(1, e)
        return (e if d > 0 else 1) if inner else (0 if d > 0 else e + 1)

    def slab(a, step, inner):
        return (a, 1, span(step[0], inner), span(step[1], inner))

    def flat_copy(a, k):
        step = flat[k]
        return pltpu.make_async_remote_copy(
            src_ref=pad.at[slab(a, step, True)], dst_ref=pad.at[slab(a, step, False)],
            send_sem=psend.at[a, k], recv_sem=precv.at[a, k],
            device_id=near[step][1], device_id_type=MESH,
        )

    def upright_copy(a, k):
        return pltpu.make_async_remote_copy(
            src_ref=zs.at[k, a], dst_ref=zr.at[k, a],
            send_sem=hsend.at[a, k], recv_sem=hrecv.at[a, k],
            device_id=near[upright[k]][1], device_id_type=MESH,
        )

    def halo_start(steps, copy, a):
        for k, step in enumerate(steps):

            @pl.when(near[step][0])
            def _(k=k):
                copy(a, k).start()

    def halo_finish(steps, copy, a):
        for k, step in enumerate(steps):
            has = near[tuple(-d for d in step)][0]

            @pl.when(has)
            def _(k=k):
                copy(a, k).wait_recv()

            @pl.when(jnp.logical_not(has))
            def _(k=k, step=step):
                if step[2]:
                    zr[k, a] = jnp.zeros((e + 2, e + 2, ch), zr.dtype)
                else:
                    shape = tuple(e for d in step[:2] if d == 0) + (e, ch)
                    pad[slab(a, step, False)] = jnp.zeros(shape, pad.dtype)

            @pl.when(near[step][0])
            def _(k=k):
                copy(a, k).wait_send()

    flat_start, flat_finish = (functools.partial(f, flat, flat_copy) for f in (halo_start, halo_finish))
    up_start, up_finish = (functools.partial(f, upright, upright_copy) for f in (halo_start, halo_finish))

    loads[2].wait()
    gather(0, f_ref)
    pl.semaphore_wait(barrier, count)
    flat_start(0)
    loads[3].wait()
    gather(1, g_ref)
    flat_start(1)
    loads[4].wait()

    zero = jnp.zeros((ch, ch), wx.dtype)

    def spread(t, carry):
        ox, oz = t // 3, lax.rem(t, 3)
        for i in range(4):
            for p in range(2):
                oy = i - p
                at = (pl.ds(i * ch, ch), pl.ds(p * ch, ch))
                if 0 <= oy <= 2:
                    wx[(0, t) + at] = w_ref[ox * 9 + oy * 3 + oz]
                    wx[(1, t) + at] = w_ref[(2 - ox) * 9 + (2 - oy) * 3 + 2 - oz].T
                else:
                    wx[(0, t) + at] = zero
                    wx[(1, t) + at] = zero
        return carry

    lax.fori_loop(0, 9, spread, 0)

    def turn(c, carry):
        for x in range(2):
            own = pad[1, 1, 2 * c + x + 1, pl.ds(1, e)].reshape(half, 2, e, ch)
            for p in range(2):
                gt[c, pl.ds(p * ch, ch), pl.ds(x * half * e, half * e)] = (
                    own[:, p].reshape(half * e, ch).T
                )
        return carry

    lax.fori_loop(0, half, turn, 0)
    flat_finish(0)

    def edges(a):
        def body(x, carry):
            v = pad[a, 1, x].astype(jnp.float32)
            zs[0, a, x] = v[:, e - 1]
            zs[1, a, x] = v[:, 0]
            return carry

        lax.fori_loop(0, e + 2, body, 0)

    edges(0)
    up_start(0)
    up_finish(0)

    zidx = lax.broadcasted_iota(jnp.int32, (1, e, 1), 1)

    def shift(a):
        def body(x, carry):
            mid = pad[a, 1, x].astype(jnp.float32)
            lo = zr[0, a, x][:, None, :]
            hi = zr[1, a, x][:, None, :]
            pad[a, 0, x] = jnp.where(zidx == 0, lo, pltpu.roll(mid, 1, 1)).astype(pad.dtype)
            pad[a, 2, x] = jnp.where(zidx == e - 1, hi, pltpu.roll(mid, e - 1, 1)).astype(pad.dtype)
            return carry

        lax.fori_loop(0, e + 2, body, 0)

    def rows(a, oz, x0, nx):
        v = pad[a, oz, pl.ds(x0, nx)].reshape(nx, half + 1, 2, e, ch)
        parts = [
            v[:, i // 2:i // 2 + half, i % 2].reshape(nx * half * e, ch) for i in range(4)
        ]
        return jnp.concatenate(parts, axis=1)

    def terms(t, carry):
        ox, oz = t // 3, lax.rem(t, 3)
        acc = jnp.zeros((2 * ch, 4 * ch), jnp.float32)
        for c in range(half):
            acc = acc + jnp.dot(
                gt[c], rows(0, oz, ox + 2 * c, 2), preferred_element_type=jnp.float32
            )
        for oy in range(3):
            block = acc[:ch, oy * ch:(oy + 1) * ch] + acc[ch:, (oy + 1) * ch:(oy + 2) * ch]
            src[pl.ds((ox * 9 + oy * 3 + oz) * tap, tap)] = block.T.reshape(tap, TILE, ch)
        return carry

    def to_mate(source, target, send, recv, mate):
        return pltpu.make_async_remote_copy(
            src_ref=source, dst_ref=target, send_sem=send, recv_sem=recv,
            device_id=mate, device_id_type=MESH,
        )

    def parts(s):
        base, size = groups[s]
        return base, size // 2, size // 2 // blk

    def core_copy(s):
        base, half_size, _ = parts(s)
        return to_mate(
            src.at[pl.ds(base + (1 - core_bit) * half_size, half_size)],
            land.at[pl.ds(base // 2, half_size)], csend.at[0, s], crecv.at[0, s], core,
        )

    def block_copy(s, r):
        size = pl.ds(0, parts(s)[2] + 1)
        return to_mate(
            qs.at[s, r, size], ql.at[s, r, size], rsend.at[s, r], rrecv.at[s, r], peers[r][1]
        )

    def far_copy(s, k):
        size = pl.ds(0, parts(s)[2] + 1)
        return to_mate(fs.at[s, k, size], fl.at[s, k, size], fsend.at[s, k], frecv.at[s, k], far[k][1])

    def gather_copy(s, r):
        size = pl.ds(0, parts(s)[2] + 1)
        return to_mate(
            aq.at[s, 0, size], aq.at[s, r, size], gsend.at[s, r], grecv.at[s, r], peers[r][1]
        )

    def back_copy(s):
        return to_mate(aq.at[s], cq.at[s], csend.at[1, s], crecv.at[1, s], core)

    def encode(v):
        top = jnp.max(jnp.abs(v), axis=0)
        power = jnp.clip(jnp.ceil(jnp.log2(top)), -126.0, 126.0)
        code = jnp.round(v * jnp.exp2(-power) * LEVELS)
        return code.astype(jnp.int32).astype(jnp.int16), power.astype(jnp.int32).astype(jnp.int16)

    def decode(code, power):
        scale = jnp.exp2(power.astype(jnp.int32).astype(jnp.float32))
        return code.astype(jnp.int32).astype(jnp.float32) * (1.0 / LEVELS) * scale

    def put_code(ref, size, v):
        code, power = encode(v)
        ref[pl.ds(0, size)] = code
        ref[size] = power

    def get_code(ref, size):
        return decode(ref[pl.ds(0, size)], ref[size])

    def begin(s):
        core_copy(s).start()

    def split(s):
        base, half_size, size = parts(s)
        core_copy(s).wait()
        order = sorted(range(1, blk), key=lambda r: -bin(r).count("1")) + [0]
        for r in order:
            at = peers[r][0] * size
            v = src[pl.ds(base + core_bit * half_size + at, size)] + land[pl.ds(base // 2 + at, size)]
            if r == 0:
                own[s, pl.ds(0, size)] = v
            else:
                put_code(qs.at[s, r], size, v)
                block_copy(s, r).start()

    def spread_out(s, v):
        put_code(aq.at[s, 0], parts(s)[2], v * factor)
        for r in sorted(range(1, blk), key=lambda r: -bin(r).count("1")):
            gather_copy(s, r).start()

    def join(s):
        size = parts(s)[2]
        v = own[s, pl.ds(0, size)]
        for r in range(1, blk):
            block_copy(s, r).wait()
            v = v + get_code(ql.at[s, r], size)
        if far:
            put_code(fs.at[s, 0], size, v)
            far_copy(s, 0).start()
        else:
            spread_out(s, v)

    def cross(s, k):
        size = parts(s)[2]
        far_copy(s, k).wait()
        mine, theirs = fs[s, k, pl.ds(0, size + 1)].astype(jnp.int32), fl[s, k, pl.ds(0, size + 1)].astype(jnp.int32)
        low = jnp.where(far[k][0] == 0, mine, theirs)
        high = jnp.where(far[k][0] == 0, theirs, mine)
        v = decode(low[:size], low[size]) + decode(high[:size], high[size])
        if k + 1 < len(far):
            put_code(fs.at[s, k + 1], size, v)
            far_copy(s, k + 1).start()
        else:
            spread_out(s, v)

    def relay(s):
        for r in range(1, blk):
            gather_copy(s, r).wait()
        back_copy(s).start()
        unpack(s, aq, core_bit, [peers[r][0] for r in range(blk)])

    def unpack(s, ref, bit, ranks):
        base, half_size, size = parts(s)
        for r in range(blk):
            dw_ref[pl.ds(base + bit * half_size + ranks[r] * size, size)] = get_code(ref.at[s, r], size)

    def close(s):
        back_copy(s).wait()
        unpack(s, cq, 1 - core_bit, [peers[r][0] for r in range(blk)])

    nx = 4

    def conv(a, c):
        x0 = c * nx
        acc = jnp.zeros((nx * half * e, 2 * ch), jnp.float32)
        for t in range(9):
            acc = acc + jnp.dot(
                rows(a, t % 3, x0 + t // 3, nx), wx[a, t], preferred_element_type=jnp.float32
            )
        for p in range(2):
            obuf[a, pl.ds(x0, nx), :, p] = (
                acc[:, p * ch:(p + 1) * ch].reshape(nx, half, 2, BE, ch).astype(obuf.dtype)
            )

    def put(a, dst):
        for s in range(8):
            p = pos_ref[0, s]
            v = obuf[
                a, pl.ds(p // 4 * BE, BE), pl.ds(lax.rem(p // 2, 2) * (BE // 2), BE // 2), :,
                lax.rem(p, 2),
            ].reshape(BE, BE, BE, ch)
            dst[s] = jnp.where(s < cnt_ref[0, 0], v, jnp.zeros_like(v))

    work = []
    for a, dst in ((0, out_ref), (1, dx_ref)):
        if a == 1:
            work.append(functools.partial(up_finish, 1))
            work.append(functools.partial(shift, 1))
        for c in range(e // nx):
            work.append(functools.partial(conv, a, c))
        work.append(functools.partial(put, a, dst))

    shift(0)
    used = 27 * tap
    if src.shape[0] > used:
        src[pl.ds(used, src.shape[0] - used)] = jnp.zeros((src.shape[0] - used, TILE, ch), src.dtype)
    early = min(3 * -(-groups[1][0] // (9 * tap)), 8)
    lax.fori_loop(0, early, terms, 0)
    begin(0)
    flat_finish(1)
    edges(1)
    up_start(1)
    lax.fori_loop(early, 8, terms, 0)
    split(0)
    lax.fori_loop(8, 9, terms, 0)
    begin(1)

    def do(n):
        for _ in range(n):
            if work:
                work.pop(0)()

    do(1)
    split(1)
    do(4)
    join(0)
    do(3)
    join(1)
    do(2)
    steps = [functools.partial(cross, s, k) for k in range(len(far)) for s in range(2)]
    for step in steps[:1]:
        step()
    do(2)
    for step in steps[1:]:
        step()
    do(len(work))
    relay(0)
    close(0)
    relay(1)
    close(1)


def leave(rows, *refs):
    sources, targets, sem = refs[:3], refs[3:6], refs[6]
    copies = [
        pltpu.make_async_copy(
            source.at[pl.ds(0, rows)] if k == 2 else source, target, sem.at[k]
        )
        for k, (source, target) in enumerate(zip(sources, targets))
    ]
    for copy in copies[::-1]:
        copy.start()
    for copy in copies:
        copy.wait()


def fused(features, cotangent, weight, pos, cnt, factor, n_tomo, n_brick):
    slots, vox, ch = features.shape
    e = 2 * BE
    half = e // 2
    n = n_tomo * n_brick
    tb, bb = n_tomo.bit_length() - 1, n_brick.bit_length() - 1
    blk = 1 << (tb + 1)
    unit = 2 * blk
    units = -(-weight.shape[0] * (ch // TILE) // unit)
    first = units // 2
    groups = [(0, first * unit), (first * unit, (units - first) * unit)]
    total = units * unit
    piece = (units - first) + 1
    far = max(bb - 2, 1)
    vm = pl.BlockSpec(memory_space=pltpu.VMEM)
    hbm = pl.BlockSpec(memory_space=pl.ANY)
    brick = jax.ShapeDtypeStruct((slots, BE, BE, BE, ch), jnp.bfloat16)
    dma = pltpu.SemaphoreType.DMA
    taps = weight.shape[0] * ch // TILE
    results = pl.pallas_call(
        functools.partial(kernel, factor, tb, bb, groups),
        out_shape=(
            pltpu.VMEM(brick.shape, jnp.bfloat16), pltpu.VMEM(brick.shape, jnp.bfloat16),
            pltpu.VMEM((total, TILE, ch), jnp.float32),
        ),
        in_specs=[pl.BlockSpec(memory_space=pltpu.HBM)] * 5,
        out_specs=(vm, vm, vm),
        scratch_shapes=[
            pltpu.SMEM(pos.shape, jnp.int32), pltpu.SMEM(cnt.shape, jnp.int32),
            pltpu.VMEM(brick.shape, jnp.bfloat16), pltpu.VMEM(brick.shape, jnp.bfloat16),
            pltpu.VMEM(weight.shape, jnp.bfloat16),
            pltpu.VMEM((2, 3, e + 2, e + 2, e, ch), jnp.bfloat16),
            pltpu.VMEM((2, 2, e + 2, e + 2, ch), jnp.float32),
            pltpu.VMEM((2, 2, e + 2, e + 2, ch), jnp.float32),
            pltpu.VMEM((2, 9, 4 * ch, 2 * ch), jnp.bfloat16),
            pltpu.VMEM((half, 2 * ch, 2 * half * e), jnp.bfloat16),
            pltpu.VMEM((2, e, half, 2, 2, BE, ch), jnp.bfloat16),
            pltpu.VMEM((total, TILE, ch), jnp.float32),
            pltpu.VMEM((total // 2, TILE, ch), jnp.float32),
            pltpu.VMEM((2, piece - 1, TILE, ch), jnp.float32),
            pltpu.VMEM((2, blk, piece, TILE, ch), jnp.int16),
            pltpu.VMEM((2, blk, piece, TILE, ch), jnp.int16),
            pltpu.VMEM((2, far, piece, TILE, ch), jnp.int16),
            pltpu.VMEM((2, far, piece, TILE, ch), jnp.int16),
            pltpu.VMEM((2, blk, piece, TILE, ch), jnp.int16),
            pltpu.VMEM((2, blk, piece, TILE, ch), jnp.int16),
            dma((5,)), dma((2, 2)), dma((2, 2)), dma((2, 8)), dma((2, 8)), dma((2, 2)), dma((2, 2)),
            dma((2, blk)), dma((2, blk)), dma((2, far)), dma((2, far)), dma((2, blk)), dma((2, blk)),
        ],
        compiler_params=pltpu.CompilerParams(
            collective_id=0, has_side_effects=True, vmem_limit_bytes=59 << 20
        ),
        name="fused",
    )(
        pos, cnt,
        features.reshape(slots, BE, BE, BE, ch), cotangent.reshape(slots, BE, BE, BE, ch), weight,
    )
    out, dx, dw = pl.pallas_call(
        functools.partial(leave, taps),
        out_shape=(brick, brick, jax.ShapeDtypeStruct((taps, TILE, ch), jnp.float32)),
        in_specs=[hbm] * 3,
        out_specs=(hbm,) * 3,
        scratch_shapes=[dma((3,))],
        compiler_params=pltpu.CompilerParams(vmem_limit_bytes=1 << 20),
        name="leave",
    )(*results)
    return out, dx, dw.reshape(weight.shape)


def shards(features, weight, cotangent, brick_pos, brick_count):
    slots, vox, ch = features.shape[1:]
    n_tomo, n_brick = lax.axis_size("tomo"), lax.axis_size("brick")
    factor = 1.0 / math.sqrt(n_tomo * n_brick * slots * vox)
    out, dx, dw = fused(
        features[0], cotangent[0], weight, brick_pos, brick_count, factor, n_tomo, n_brick
    )
    return out.reshape(1, slots, vox, ch), dx.reshape(1, slots, vox, ch), dw


def solution(mesh):
    in_specs = (
        P("tomo", "brick", None, None),
        P(),
        P("tomo", "brick", None, None),
        P("tomo", "brick"),
        P("tomo", "brick"),
    )
    out_specs = (P("tomo", "brick", None, None), P("tomo", "brick", None, None), P())
    return jax.shard_map(shards, mesh=mesh, in_specs=in_specs, out_specs=out_specs, check_vma=False)
```

```python
import functools
import math

import jax
import jax.numpy as jnp
from jax import lax
from jax.experimental import pallas as pl
from jax.experimental.pallas import tpu as pltpu
from jax.sharding import PartitionSpec as P

BE = 8
MESH = pl.DeviceIdType.MESH
TILE = 16
LEVELS = 32000.0
PAIR = 2


def coords_of(index, levels):
    out = []
    for bit in (2, 1, 0):
        c = 0
        for level in range(levels):
            c = c + lax.rem(index // (1 << (3 * level + bit)), 2) * (1 << level)
        out.append(c)
    return out


def index_of(coords, levels):
    i = 0
    for bit, c in zip((2, 1, 0), coords):
        for level in range(levels):
            i = i + lax.rem(c // (1 << level), 2) * (1 << (3 * level + bit))
    return i


def kernel(
    factor, tb, bb, groups,
    pos_hbm, cnt_hbm, f_hbm, g_hbm, w_hbm,
    out_ref, dx_ref, dw_ref,
    pos_ref, cnt_ref, f_ref, g_ref, w_ref, pad, zs, zr, lx, ly, rs, rr, wx, gt, gy, gx, obuf, src, land, own, qs, ql, fs, fl, aq, cq,
    isem, hsend, hrecv, psend, precv, esend, erecv, csend, crecv, rsend, rrecv, fsend, frecv, gsend, grecv,
):
    e = 2 * BE
    half = e // 2
    lane = half * e
    ch = f_ref.shape[-1]
    tap = ch // TILE
    levels = bb // 3
    side = 1 << levels
    tomo = lax.axis_index("tomo")
    brick = lax.axis_index("brick")
    here = coords_of(brick, levels)

    loads = [
        pltpu.make_async_copy(source, target, isem.at[k])
        for k, (source, target) in enumerate((
            (pos_hbm, pos_ref), (cnt_hbm, cnt_ref), (f_hbm, f_ref), (g_hbm, g_ref), (w_hbm, w_ref)
        ))
    ]
    for load in loads:
        load.start()

    def neighbour(step):
        at, has = [], True
        for c, d in zip(here, step):
            at.append(lax.rem(c + d + side, side))
            if d:
                has = jnp.logical_and(has, c < side - 1 if d > 0 else c > 0)
        return has, (tomo, index_of(at, levels))

    flat = [(i, j, 0) for i in (-1, 0, 1) for j in (-1, 0, 1) if i or j]
    upright = [(0, 0, 1), (0, 0, -1)]
    near = {step: neighbour(step) for step in flat + upright}

    def mate_on(v, width):
        bit = lax.rem(v // width, 2)
        return bit, v + width - 2 * width * bit

    core_bit, core_mate = mate_on(brick, 1)
    core = (tomo, core_mate)
    flips = [(0, 1 << k) for k in range(tb)] + [(1, 2)]
    blk = 1 << len(flips)
    home = 0
    for k, (axis, width) in enumerate(flips):
        home = home + lax.rem((tomo, brick)[axis] // width, 2) * (1 << k)
    peers = []
    for r in range(blk):
        at, rank = [tomo, brick], home
        for k, (axis, width) in enumerate(flips):
            if r >> k & 1:
                at[axis] = mate_on(at[axis], width)[1]
                rank = mate_on(rank, 1 << k)[1]
        peers.append((rank, tuple(at)))
    far = []
    for k in range(2, bb):
        bit, mate = mate_on(brick, 1 << k)
        far.append((bit, (tomo, mate)))

    barrier = pltpu.get_barrier_semaphore()
    greet = [core] + [mate for _, mate in peers[1:]] + [mate for _, mate in far]
    count = len(greet)
    for mate in greet:
        pl.semaphore_signal(barrier, inc=1, device_id=mate, device_id_type=MESH)
    for has, mate in near.values():

        @pl.when(has)
        def _(mate=mate):
            pl.semaphore_signal(barrier, inc=1, device_id=mate, device_id_type=MESH)

        count = count + has.astype(jnp.int32)

    loads[0].wait()
    loads[1].wait()

    slots = []
    for p in range(8):
        s = jnp.int32(0)
        for k in range(8):
            s = jnp.where(pos_ref[0, k] == p, k, s)
        slots.append(s)

    def gather(a, ref):
        def body(x, carry):
            for q in range(4):
                parts = []
                for pz in range(2):
                    s = slots[2 * q + pz]
                    v = ref[s, x].astype(jnp.float32)
                    parts.append(jnp.where(s < cnt_ref[0, 0], v, 0.0))
                v = jnp.concatenate(parts, axis=1)
                at, y = q // 2 * BE + x, q % 2 * BE
                pad[a, 1, 1 + at, pl.ds(1 + y, BE)] = v.astype(pad.dtype)
                zs[0, a, at, pl.ds(y, BE)] = v[:, e - 1]
                zs[1, a, at, pl.ds(y, BE)] = v[:, 0]
            return carry

        lax.fori_loop(0, BE, body, 0)

    def inner(d):
        return pl.ds(1, e) if d == 0 else e if d > 0 else 1

    def landing(a, step):
        if step[0] == 0:
            return ly, (a, 0 if step[1] > 0 else 1)
        side = 0 if step[0] > 0 else 1
        return lx, (a, side, pl.ds(1, e) if step[1] == 0 else 0 if step[1] > 0 else e + 1)

    def flat_copy(a, k):
        step = flat[k]
        ref, at = landing(a, step)
        return pltpu.make_async_remote_copy(
            src_ref=pad.at[a, 1, inner(step[0]), inner(step[1])], dst_ref=ref.at[at],
            send_sem=psend.at[a, k], recv_sem=precv.at[a, k],
            device_id=near[step][1], device_id_type=MESH,
        )

    def ring_copy(a, k):
        return pltpu.make_async_remote_copy(
            src_ref=rs.at[k, a], dst_ref=rr.at[k, a],
            send_sem=esend.at[a, k], recv_sem=erecv.at[a, k],
            device_id=near[upright[k]][1], device_id_type=MESH,
        )

    def upright_copy(a, k):
        return pltpu.make_async_remote_copy(
            src_ref=zs.at[k, a], dst_ref=zr.at[k, a],
            send_sem=hsend.at[a, k], recv_sem=hrecv.at[a, k],
            device_id=near[upright[k]][1], device_id_type=MESH,
        )

    def halo_start(steps, copy, a):
        for k, step in enumerate(steps):

            @pl.when(near[step][0])
            def _(k=k):
                copy(a, k).start()

    def halo_finish(steps, copy, clear, a):
        for k, step in enumerate(steps):
            has = near[tuple(-d for d in step)][0]

            @pl.when(has)
            def _(k=k):
                copy(a, k).wait_recv()

            @pl.when(jnp.logical_not(has))
            def _(k=k):
                clear(a, k)

            @pl.when(near[step][0])
            def _(k=k):
                copy(a, k).wait_send()

    def flat_clear(a, k):
        ref, at = landing(a, flat[k])
        shape = tuple(e for d in flat[k][:2] if d == 0) + (e, ch)
        ref[at] = jnp.zeros(shape, ref.dtype)

    def up_clear(a, k):
        zr[k, a] = jnp.zeros((e, e, ch), zr.dtype)

    def ring_clear(a, k):
        rr[k, a] = jnp.zeros(rr.shape[2:], rr.dtype)

    flat_start = functools.partial(halo_start, flat, flat_copy)
    flat_finish = functools.partial(halo_finish, flat, flat_copy, flat_clear)
    up_start = functools.partial(halo_start, upright, upright_copy)
    up_finish = functools.partial(halo_finish, upright, upright_copy, up_clear)
    ring_start = functools.partial(halo_start, upright, ring_copy)
    ring_finish = functools.partial(halo_finish, upright, ring_copy, ring_clear)

    loads[2].wait()
    gather(0, f_ref)
    loads[3].wait()
    gather(1, g_ref)
    loads[4].wait()

    zero = jnp.zeros((ch, ch), wx.dtype)

    def spread(t, carry):
        ox, oz = t // 3, lax.rem(t, 3)
        for i in range(4):
            for p in range(2):
                oy = i - p
                at = (pl.ds(i * ch, ch), pl.ds(p * ch, ch))
                if 0 <= oy <= 2:
                    wx[(0, t) + at] = w_ref[ox * 9 + oy * 3 + oz]
                    wx[(1, t) + at] = w_ref[(2 - ox) * 9 + (2 - oy) * 3 + 2 - oz].T
                else:
                    wx[(0, t) + at] = zero
                    wx[(1, t) + at] = zero
        return carry

    def turn(x, carry):
        v = pad[1, 1, x + 1, pl.ds(1, e)].reshape(half, 2, e, ch)
        at = pl.ds(pl.multiple_of((x + 1) * lane, lane), lane)
        for p in range(2):
            gt[pl.ds(p * ch, ch), at] = v[:, p].reshape(lane, ch).T
        return carry

    def empty(oz, carry):
        for x in (0, e + 1):
            pad[0, oz, x] = jnp.zeros((e + 2, e, ch), pad.dtype)
        for y in (0, e + 1):
            pad[0, oz, pl.ds(1, e), y] = jnp.zeros((e, e, ch), pad.dtype)
        return carry

    lax.fori_loop(0, 3, empty, 0)
    lax.fori_loop(0, e, turn, 0)
    blank = jnp.zeros((2 * ch, lane), gt.dtype)
    gt[:, pl.ds(0, lane)] = blank
    gt[:, pl.ds((e + 1) * lane, lane)] = blank
    nil = jnp.zeros((1, e, ch), pad.dtype)
    for p, y in ((0, 1), (1, e)):
        v = pad[1, 1, pl.ds(1, e), y]
        for ox, kept in enumerate((
            jnp.concatenate([v[1:], nil], axis=0), v, jnp.concatenate([nil, v[:e - 1]], axis=0)
        )):
            gy[pl.ds((2 * ox + p) * ch, ch)] = kept.reshape(e * e, ch).T
    for k, x in ((0, 1), (1, e)):
        gx[pl.ds(2 * k * ch, 2 * ch), pl.ds(k * lane, lane)] = gt[:, pl.ds(x * lane, lane)]
        gx[pl.ds(2 * k * ch, 2 * ch), pl.ds((1 - k) * lane, lane)] = blank
    pl.semaphore_wait(barrier, count)
    up_start(0)
    flat_start(0)
    up_start(1)
    flat_start(1)
    up_finish(0)

    def ring(a):
        for k, z in ((0, e - 1), (1, 0)):
            for side in range(2):
                rs[k, a, side, pl.ds(0, e + 2)] = lx[a, side].astype(jnp.float32)[:, z]
                rs[k, a, 2 + side, pl.ds(0, e)] = ly[a, side].astype(jnp.float32)[:, z]

    zidx = lax.broadcasted_iota(jnp.int32, (1, e, 1), 1)

    def slide(mid, lo, hi):
        below = jnp.where(zidx == 0, lo[:, None, :], pltpu.roll(mid, 1, 1))
        above = jnp.where(zidx == e - 1, hi[:, None, :], pltpu.roll(mid, e - 1, 1))
        return below.astype(pad.dtype), above.astype(pad.dtype)

    def shift(a):
        def body(x, carry):
            mid = pad[a, 1, x + 1, pl.ds(1, e)].astype(jnp.float32)
            below, above = slide(mid, zr[0, a, x], zr[1, a, x])
            pad[a, 0, x + 1, pl.ds(1, e)] = below
            pad[a, 2, x + 1, pl.ds(1, e)] = above
            return carry

        lax.fori_loop(0, e, body, 0)

    def lay(a):
        for side, at in ((0, 0), (1, e + 1)):
            pad[a, 1, at] = lx[a, side]
            pad[a, 1, pl.ds(1, e), at] = ly[a, side]

    def fill(a):
        for side, at in ((0, 0), (1, e + 1)):
            mid = lx[a, side]
            below, above = slide(
                mid.astype(jnp.float32), rr[0, a, side, pl.ds(0, e + 2)], rr[1, a, side, pl.ds(0, e + 2)]
            )
            for oz, v in ((0, below), (2, above)):
                pad[a, oz, at] = v
            mid = ly[a, side]
            below, above = slide(
                mid.astype(jnp.float32), rr[0, a, 2 + side, pl.ds(0, e)], rr[1, a, 2 + side, pl.ds(0, e)]
            )
            for oz, v in ((0, below), (2, above)):
                pad[a, oz, pl.ds(1, e), at] = v

    def rows(a, oz, x0, nx):
        v = pad[a, oz, pl.ds(x0, nx)].reshape(nx, half + 1, 2, e, ch)
        parts = [
            v[:, i // 2:i // 2 + half, i % 2].reshape(nx * half * e, ch) for i in range(4)
        ]
        return jnp.concatenate(parts, axis=1)

    def terms(oz, carry):
        acc = jnp.zeros((6 * ch, 4 * ch), jnp.float32)
        for x in range(0, e, PAIR):
            left = jnp.concatenate(
                [gt[:, (x + 2 - ox) * lane:(x + 2 - ox + PAIR) * lane] for ox in range(3)], axis=0
            )
            acc = acc + jnp.dot(left, rows(0, oz, x + 1, PAIR), preferred_element_type=jnp.float32)
        for ox in range(3):
            top = 2 * ox * ch
            for oy in range(3):
                block = (
                    acc[top:top + ch, oy * ch:(oy + 1) * ch]
                    + acc[top + ch:top + 2 * ch, (oy + 1) * ch:(oy + 2) * ch]
                )
                src[pl.ds((ox * 9 + oy * 3 + oz) * tap, tap)] = block.reshape(tap, TILE, ch)
        return carry

    def border(oz, carry):
        ends = [pad[0, oz, pl.ds(1, e), y].reshape(e * e, ch) for y in (0, e + 1)]
        sides = [rows(0, oz, x, 1) for x in (0, e + 1)]
        by_y = jnp.dot(gy[...], jnp.concatenate(ends, axis=1), preferred_element_type=jnp.float32)
        by_x = jnp.dot(gx[...], jnp.concatenate(sides, axis=0), preferred_element_type=jnp.float32)
        for ox in range(3):
            for oy in range(3):
                at = pl.ds((ox * 9 + oy * 3 + oz) * tap, tap)
                block = src[at].reshape(ch, ch)
                if oy != 1:
                    top, side = (2 * ox + oy // 2) * ch, oy // 2 * ch
                    block = block + by_y[top:top + ch, side:side + ch]
                if ox != 1:
                    top = ox * ch
                    block = block + by_x[top:top + ch, oy * ch:(oy + 1) * ch]
                    block = block + by_x[top + ch:top + 2 * ch, (oy + 1) * ch:(oy + 2) * ch]
                src[at] = block.T.reshape(tap, TILE, ch)
        return carry

    def to_mate(source, target, send, recv, mate):
        return pltpu.make_async_remote_copy(
            src_ref=source, dst_ref=target, send_sem=send, recv_sem=recv,
            device_id=mate, device_id_type=MESH,
        )

    def parts(s):
        base, size = groups[s]
        return base, size // 2, size // 2 // blk

    def core_copy(s):
        base, half_size, _ = parts(s)
        return to_mate(
            src.at[pl.ds(base + (1 - core_bit) * half_size, half_size)],
            land.at[pl.ds(base // 2, half_size)], csend.at[0, s], crecv.at[0, s], core,
        )

    def block_copy(s, r):
        size = pl.ds(0, parts(s)[2] + 1)
        return to_mate(
            qs.at[s, r, size], ql.at[s, r, size], rsend.at[s, r], rrecv.at[s, r], peers[r][1]
        )

    def far_copy(s, k):
        size = pl.ds(0, parts(s)[2] + 1)
        return to_mate(fs.at[s, k, size], fl.at[s, k, size], fsend.at[s, k], frecv.at[s, k], far[k][1])

    def gather_copy(s, r):
        size = pl.ds(0, parts(s)[2] + 1)
        return to_mate(
            aq.at[s, 0, size], aq.at[s, r, size], gsend.at[s, r], grecv.at[s, r], peers[r][1]
        )

    def back_copy(s):
        return to_mate(aq.at[s], cq.at[s], csend.at[1, s], crecv.at[1, s], core)

    def encode(v):
        top = jnp.max(jnp.abs(v), axis=0)
        power = jnp.clip(jnp.ceil(jnp.log2(top)), -126.0, 126.0)
        code = jnp.round(v * jnp.exp2(-power) * LEVELS)
        return code.astype(jnp.int32).astype(jnp.int16), power.astype(jnp.int32).astype(jnp.int16)

    def decode(code, power):
        scale = jnp.exp2(power.astype(jnp.int32).astype(jnp.float32))
        return code.astype(jnp.int32).astype(jnp.float32) * (1.0 / LEVELS) * scale

    def put_code(ref, size, v):
        code, power = encode(v)
        ref[pl.ds(0, size)] = code
        ref[size] = power

    def get_code(ref, size):
        return decode(ref[pl.ds(0, size)], ref[size])

    def begin(s):
        core_copy(s).start()

    def split(s):
        base, half_size, size = parts(s)
        core_copy(s).wait()
        order = sorted(range(1, blk), key=lambda r: -bin(r).count("1")) + [0]
        for r in order:
            at = peers[r][0] * size
            v = src[pl.ds(base + core_bit * half_size + at, size)] + land[pl.ds(base // 2 + at, size)]
            if r == 0:
                own[s, pl.ds(0, size)] = v
            else:
                put_code(qs.at[s, r], size, v)
                block_copy(s, r).start()

    def spread_out(s, v):
        put_code(aq.at[s, 0], parts(s)[2], v * factor)
        for r in sorted(range(1, blk), key=lambda r: -bin(r).count("1")):
            gather_copy(s, r).start()

    def join(s):
        size = parts(s)[2]
        v = own[s, pl.ds(0, size)]
        for r in range(1, blk):
            block_copy(s, r).wait()
            v = v + get_code(ql.at[s, r], size)
        if far:
            put_code(fs.at[s, 0], size, v)
            far_copy(s, 0).start()
        else:
            spread_out(s, v)

    def cross(s, k):
        size = parts(s)[2]
        far_copy(s, k).wait()
        mine, theirs = fs[s, k, pl.ds(0, size + 1)].astype(jnp.int32), fl[s, k, pl.ds(0, size + 1)].astype(jnp.int32)
        low = jnp.where(far[k][0] == 0, mine, theirs)
        high = jnp.where(far[k][0] == 0, theirs, mine)
        v = decode(low[:size], low[size]) + decode(high[:size], high[size])
        if k + 1 < len(far):
            put_code(fs.at[s, k + 1], size, v)
            far_copy(s, k + 1).start()
        else:
            spread_out(s, v)

    def relay(s):
        for r in range(1, blk):
            gather_copy(s, r).wait()
        back_copy(s).start()
        unpack(s, aq, core_bit, [peers[r][0] for r in range(blk)])

    def unpack(s, ref, bit, ranks):
        base, half_size, size = parts(s)
        for r in range(blk):
            dw_ref[pl.ds(base + bit * half_size + ranks[r] * size, size)] = get_code(ref.at[s, r], size)

    def close(s):
        back_copy(s).wait()
        unpack(s, cq, 1 - core_bit, [peers[r][0] for r in range(blk)])

    nx = 4

    def conv(a, c):
        x0 = c * nx
        acc = jnp.zeros((nx * half * e, 2 * ch), jnp.float32)
        for t in range(9):
            acc = acc + jnp.dot(
                rows(a, t % 3, x0 + t // 3, nx), wx[a, t], preferred_element_type=jnp.float32
            )
        for p in range(2):
            obuf[a, pl.ds(x0, nx), :, p] = (
                acc[:, p * ch:(p + 1) * ch].reshape(nx, half, 2, BE, ch).astype(obuf.dtype)
            )

    def put(a, dst):
        for s in range(8):
            p = pos_ref[0, s]
            v = obuf[
                a, pl.ds(p // 4 * BE, BE), pl.ds(lax.rem(p // 2, 2) * (BE // 2), BE // 2), :,
                lax.rem(p, 2),
            ].reshape(BE, BE, BE, ch)
            dst[s] = jnp.where(s < cnt_ref[0, 0], v, jnp.zeros_like(v))

    def ready():
        lay(1)
        ring_finish(1)
        fill(1)
        up_finish(1)
        shift(1)

    work = []
    for a, dst in ((0, out_ref), (1, dx_ref)):
        if a == 1:
            work.append(ready)
        for c in range(e // nx):
            work.append(functools.partial(conv, a, c))
        work.append(functools.partial(put, a, dst))

    shift(0)
    used = 27 * tap
    if src.shape[0] > used:
        src[pl.ds(used, src.shape[0] - used)] = jnp.zeros((src.shape[0] - used, TILE, ch), src.dtype)
    lax.fori_loop(0, 3, terms, 0)
    flat_finish(0)
    ring(0)
    ring_start(0)
    lay(0)
    border(1, 0)
    ring_finish(0)
    fill(0)
    border(0, 0)
    border(2, 0)
    begin(0)
    begin(1)
    flat_finish(1)
    ring(1)
    ring_start(1)
    lax.fori_loop(0, 9, spread, 0)

    def do(n):
        for _ in range(n):
            if work:
                work.pop(0)()

    last = len(far) - 1
    split(0)
    split(1)
    do(5)
    join(0)
    do(1)
    join(1)
    do(2)
    cross(0, last)
    do(2)
    cross(1, last)
    do(len(work))
    relay(0)
    close(0)
    relay(1)
    close(1)

def leave(rows, *refs):
    sources, targets, sem = refs[:3], refs[3:6], refs[6]
    copies = [
        pltpu.make_async_copy(
            source.at[pl.ds(0, rows)] if k == 2 else source, target, sem.at[k]
        )
        for k, (source, target) in enumerate(zip(sources, targets))
    ]
    for copy in copies[::-1]:
        copy.start()
    for copy in copies:
        copy.wait()


def fused(features, cotangent, weight, pos, cnt, factor, n_tomo, n_brick):
    slots, vox, ch = features.shape
    e = 2 * BE
    half = e // 2
    n = n_tomo * n_brick
    tb, bb = n_tomo.bit_length() - 1, n_brick.bit_length() - 1
    blk = 1 << (tb + 1)
    unit = 2 * blk
    units = -(-weight.shape[0] * (ch // TILE) // unit)
    first = units // 2
    groups = [(0, first * unit), (first * unit, (units - first) * unit)]
    total = units * unit
    piece = (units - first) + 1
    far = max(bb - 2, 1)
    vm = pl.BlockSpec(memory_space=pltpu.VMEM)
    hbm = pl.BlockSpec(memory_space=pl.ANY)
    brick = jax.ShapeDtypeStruct((slots, BE, BE, BE, ch), jnp.bfloat16)
    dma = pltpu.SemaphoreType.DMA
    taps = weight.shape[0] * ch // TILE
    results = pl.pallas_call(
        functools.partial(kernel, factor, tb, bb, groups),
        out_shape=(
            pltpu.VMEM(brick.shape, jnp.bfloat16), pltpu.VMEM(brick.shape, jnp.bfloat16),
            pltpu.VMEM((total, TILE, ch), jnp.float32),
        ),
        in_specs=[pl.BlockSpec(memory_space=pltpu.HBM)] * 5,
        out_specs=(vm, vm, vm),
        scratch_shapes=[
            pltpu.SMEM(pos.shape, jnp.int32), pltpu.SMEM(cnt.shape, jnp.int32),
            pltpu.VMEM(brick.shape, jnp.bfloat16), pltpu.VMEM(brick.shape, jnp.bfloat16),
            pltpu.VMEM(weight.shape, jnp.bfloat16),
            pltpu.VMEM((2, 3, e + 2, e + 2, e, ch), jnp.bfloat16),
            pltpu.VMEM((2, 2, e, e, ch), jnp.float32),
            pltpu.VMEM((2, 2, e, e, ch), jnp.float32),
            pltpu.VMEM((2, 2, e + 2, e, ch), jnp.bfloat16),
            pltpu.VMEM((2, 2, e, e, ch), jnp.bfloat16),
            pltpu.VMEM((2, 2, 4, e + 8, ch), jnp.float32),
            pltpu.VMEM((2, 2, 4, e + 8, ch), jnp.float32),
            pltpu.VMEM((2, 9, 4 * ch, 2 * ch), jnp.bfloat16),
            pltpu.VMEM((2 * ch, (e + 2) * half * e), jnp.bfloat16),
            pltpu.VMEM((6 * ch, e * e), jnp.bfloat16),
            pltpu.VMEM((4 * ch, e * e), jnp.bfloat16),
            pltpu.VMEM((2, e, half, 2, 2, BE, ch), jnp.bfloat16),
            pltpu.VMEM((total, TILE, ch), jnp.float32),
            pltpu.VMEM((total // 2, TILE, ch), jnp.float32),
            pltpu.VMEM((2, piece - 1, TILE, ch), jnp.float32),
            pltpu.VMEM((2, blk, piece, TILE, ch), jnp.int16),
            pltpu.VMEM((2, blk, piece, TILE, ch), jnp.int16),
            pltpu.VMEM((2, far, piece, TILE, ch), jnp.int16),
            pltpu.VMEM((2, far, piece, TILE, ch), jnp.int16),
            pltpu.VMEM((2, blk, piece, TILE, ch), jnp.int16),
            pltpu.VMEM((2, blk, piece, TILE, ch), jnp.int16),
            dma((5,)), dma((2, 2)), dma((2, 2)), dma((2, 8)), dma((2, 8)),
            dma((2, 2)), dma((2, 2)), dma((2, 2)), dma((2, 2)),
            dma((2, blk)), dma((2, blk)), dma((2, far)), dma((2, far)), dma((2, blk)), dma((2, blk)),
        ],
        compiler_params=pltpu.CompilerParams(
            collective_id=0, has_side_effects=True, vmem_limit_bytes=59 << 20
        ),
        name="fused",
    )(
        pos, cnt,
        features.reshape(slots, BE, BE, BE, ch), cotangent.reshape(slots, BE, BE, BE, ch), weight,
    )
    out, dx, dw = pl.pallas_call(
        functools.partial(leave, taps),
        out_shape=(brick, brick, jax.ShapeDtypeStruct((taps, TILE, ch), jnp.float32)),
        in_specs=[hbm] * 3,
        out_specs=(hbm,) * 3,
        scratch_shapes=[dma((3,))],
        compiler_params=pltpu.CompilerParams(vmem_limit_bytes=1 << 20),
        name="leave",
    )(*results)
    return out, dx, dw.reshape(weight.shape)


def shards(features, weight, cotangent, brick_pos, brick_count):
    slots, vox, ch = features.shape[1:]
    n_tomo, n_brick = lax.axis_size("tomo"), lax.axis_size("brick")
    factor = 1.0 / math.sqrt(n_tomo * n_brick * slots * vox)
    out, dx, dw = fused(
        features[0], cotangent[0], weight, brick_pos, brick_count, factor, n_tomo, n_brick
    )
    return out.reshape(1, slots, vox, ch), dx.reshape(1, slots, vox, ch), dw


def solution(mesh):
    in_specs = (
        P("tomo", "brick", None, None),
        P(),
        P("tomo", "brick", None, None),
        P("tomo", "brick"),
        P("tomo", "brick"),
    )
    out_specs = (P("tomo", "brick", None, None), P("tomo", "brick", None, None), P())
    return jax.shard_map(shards, mesh=mesh, in_specs=in_specs, out_specs=out_specs, check_vma=False)
```

```python
import functools
import math

import jax
import jax.numpy as jnp
from jax import lax
from jax.experimental import pallas as pl
from jax.experimental.pallas import tpu as pltpu
from jax.sharding import PartitionSpec as P

BE = 8
MESH = pl.DeviceIdType.MESH
TILE = 16
LEVELS = 32000.0
PAIR = 2


def coords_of(index, levels):
    out = []
    for bit in (2, 1, 0):
        c = 0
        for level in range(levels):
            c = c + lax.rem(index // (1 << (3 * level + bit)), 2) * (1 << level)
        out.append(c)
    return out


def index_of(coords, levels):
    i = 0
    for bit, c in zip((2, 1, 0), coords):
        for level in range(levels):
            i = i + lax.rem(c // (1 << level), 2) * (1 << (3 * level + bit))
    return i


def kernel(
    factor, tb, bb, groups,
    pos_hbm, cnt_hbm, f_hbm, g_hbm, w_hbm,
    out_ref, dx_ref, dw_ref,
    pos_ref, cnt_ref, f_ref, g_ref, w_ref, pad, zs, zr, lx, ly, rs, rr, wx, gt, gy, gx, obuf, src, land, own, qs, ql, fs, fl, aq, cq,
    isem, hsend, hrecv, psend, precv, esend, erecv, csend, crecv, bsend, brecv, rsend, rrecv, fsend, frecv, gsend, grecv,
):
    e = 2 * BE
    half = e // 2
    lane = half * e
    ch = f_ref.shape[-1]
    tap = ch // TILE
    levels = bb // 3
    side = 1 << levels
    tomo = lax.axis_index("tomo")
    brick = lax.axis_index("brick")
    here = coords_of(brick, levels)

    loads = [
        pltpu.make_async_copy(source, target, isem.at[k])
        for k, (source, target) in enumerate((
            (pos_hbm, pos_ref), (cnt_hbm, cnt_ref), (f_hbm, f_ref), (g_hbm, g_ref), (w_hbm, w_ref)
        ))
    ]
    for load in loads:
        load.start()

    def neighbour(step):
        at, has = [], True
        for c, d in zip(here, step):
            at.append(lax.rem(c + d + side, side))
            if d:
                has = jnp.logical_and(has, c < side - 1 if d > 0 else c > 0)
        return has, (tomo, index_of(at, levels))

    flat = [(i, j, 0) for i in (-1, 0, 1) for j in (-1, 0, 1) if i or j]
    upright = [(0, 0, 1), (0, 0, -1)]
    near = {step: neighbour(step) for step in flat + upright}

    def mate_on(v, width):
        bit = lax.rem(v // width, 2)
        return bit, v + width - 2 * width * bit

    core_bit, core_mate = mate_on(brick, 1)
    core = (tomo, core_mate)
    flips = [(0, 1 << k) for k in range(tb)] + [(1, 2)]
    blk = 1 << len(flips)
    home = 0
    for k, (axis, width) in enumerate(flips):
        home = home + lax.rem((tomo, brick)[axis] // width, 2) * (1 << k)
    peers = []
    for r in range(blk):
        at, rank = [tomo, brick], home
        for k, (axis, width) in enumerate(flips):
            if r >> k & 1:
                at[axis] = mate_on(at[axis], width)[1]
                rank = mate_on(rank, 1 << k)[1]
        peers.append((rank, tuple(at)))
    far = []
    for k in range(2, bb):
        bit, mate = mate_on(brick, 1 << k)
        far.append((bit, (tomo, mate)))

    barrier = pltpu.get_barrier_semaphore()
    greet = [core] + [mate for _, mate in peers[1:]] + [mate for _, mate in far]
    count = len(greet)
    for mate in greet:
        pl.semaphore_signal(barrier, inc=1, device_id=mate, device_id_type=MESH)
    for has, mate in near.values():

        @pl.when(has)
        def _(mate=mate):
            pl.semaphore_signal(barrier, inc=1, device_id=mate, device_id_type=MESH)

        count = count + has.astype(jnp.int32)

    loads[0].wait()
    loads[1].wait()

    slots = []
    for p in range(8):
        s = jnp.int32(0)
        for k in range(8):
            s = jnp.where(pos_ref[0, k] == p, k, s)
        slots.append(s)

    def gather(a, ref):
        def body(x, carry):
            for q in range(4):
                parts = []
                for pz in range(2):
                    s = slots[2 * q + pz]
                    v = ref[s, x].astype(jnp.float32)
                    parts.append(jnp.where(s < cnt_ref[0, 0], v, 0.0))
                v = jnp.concatenate(parts, axis=1)
                at, y = q // 2 * BE + x, q % 2 * BE
                pad[a, 1, 1 + at, pl.ds(1 + y, BE)] = v.astype(pad.dtype)
                zs[0, a, at, pl.ds(y, BE)] = v[:, e - 1]
                zs[1, a, at, pl.ds(y, BE)] = v[:, 0]
            return carry

        lax.fori_loop(0, BE, body, 0)

    def inner(d):
        return pl.ds(1, e) if d == 0 else e if d > 0 else 1

    def landing(a, step):
        if step[0] == 0:
            return ly, (a, 0 if step[1] > 0 else 1)
        side = 0 if step[0] > 0 else 1
        return lx, (a, side, pl.ds(1, e) if step[1] == 0 else 0 if step[1] > 0 else e + 1)

    def flat_copy(a, k):
        step = flat[k]
        ref, at = landing(a, step)
        return pltpu.make_async_remote_copy(
            src_ref=pad.at[a, 1, inner(step[0]), inner(step[1])], dst_ref=ref.at[at],
            send_sem=psend.at[a, k], recv_sem=precv.at[a, k],
            device_id=near[step][1], device_id_type=MESH,
        )

    def ring_copy(a, k):
        return pltpu.make_async_remote_copy(
            src_ref=rs.at[k, a], dst_ref=rr.at[k, a],
            send_sem=esend.at[a, k], recv_sem=erecv.at[a, k],
            device_id=near[upright[k]][1], device_id_type=MESH,
        )

    def upright_copy(a, k):
        return pltpu.make_async_remote_copy(
            src_ref=zs.at[k, a], dst_ref=zr.at[k, a],
            send_sem=hsend.at[a, k], recv_sem=hrecv.at[a, k],
            device_id=near[upright[k]][1], device_id_type=MESH,
        )

    def halo_start(steps, copy, a):
        for k, step in enumerate(steps):

            @pl.when(near[step][0])
            def _(k=k):
                copy(a, k).start()

    def halo_finish(steps, copy, clear, a):
        for k, step in enumerate(steps):
            has = near[tuple(-d for d in step)][0]

            @pl.when(has)
            def _(k=k):
                copy(a, k).wait_recv()

            @pl.when(jnp.logical_not(has))
            def _(k=k):
                clear(a, k)

            @pl.when(near[step][0])
            def _(k=k):
                copy(a, k).wait_send()

    def flat_clear(a, k):
        ref, at = landing(a, flat[k])
        shape = tuple(e for d in flat[k][:2] if d == 0) + (e, ch)
        ref[at] = jnp.zeros(shape, ref.dtype)

    def up_clear(a, k):
        zr[k, a] = jnp.zeros((e, e, ch), zr.dtype)

    def ring_clear(a, k):
        rr[k, a] = jnp.zeros(rr.shape[2:], rr.dtype)

    flat_start = functools.partial(halo_start, flat, flat_copy)
    flat_finish = functools.partial(halo_finish, flat, flat_copy, flat_clear)
    up_start = functools.partial(halo_start, upright, upright_copy)
    up_finish = functools.partial(halo_finish, upright, upright_copy, up_clear)
    ring_start = functools.partial(halo_start, upright, ring_copy)
    ring_finish = functools.partial(halo_finish, upright, ring_copy, ring_clear)

    loads[2].wait()
    gather(0, f_ref)
    loads[3].wait()
    gather(1, g_ref)
    loads[4].wait()

    zero = jnp.zeros((ch, ch), wx.dtype)

    def spread(t, carry):
        ox, oz = t // 3, lax.rem(t, 3)
        for i in range(4):
            for p in range(2):
                oy = i - p
                at = (pl.ds(i * ch, ch), pl.ds(p * ch, ch))
                if 0 <= oy <= 2:
                    wx[(0, t) + at] = w_ref[ox * 9 + oy * 3 + oz]
                    wx[(1, t) + at] = w_ref[(2 - ox) * 9 + (2 - oy) * 3 + 2 - oz].T
                else:
                    wx[(0, t) + at] = zero
                    wx[(1, t) + at] = zero
        return carry

    def turn(x, carry):
        v = pad[1, 1, x + 1, pl.ds(1, e)].reshape(half, 2, e, ch)
        at = pl.ds(pl.multiple_of((x + 1) * lane, lane), lane)
        for p in range(2):
            gt[pl.ds(p * ch, ch), at] = v[:, p].reshape(lane, ch).T
        return carry

    def empty(oz, carry):
        for x in (0, e + 1):
            pad[0, oz, x] = jnp.zeros((e + 2, e, ch), pad.dtype)
        for y in (0, e + 1):
            pad[0, oz, pl.ds(1, e), y] = jnp.zeros((e, e, ch), pad.dtype)
        return carry

    lax.fori_loop(0, 3, empty, 0)
    lax.fori_loop(0, e, turn, 0)
    blank = jnp.zeros((2 * ch, lane), gt.dtype)
    gt[:, pl.ds(0, lane)] = blank
    gt[:, pl.ds((e + 1) * lane, lane)] = blank
    nil = jnp.zeros((1, e, ch), pad.dtype)
    for p, y in ((0, 1), (1, e)):
        v = pad[1, 1, pl.ds(1, e), y]
        for ox, kept in enumerate((
            jnp.concatenate([v[1:], nil], axis=0), v, jnp.concatenate([nil, v[:e - 1]], axis=0)
        )):
            gy[pl.ds((2 * ox + p) * ch, ch)] = kept.reshape(e * e, ch).T
    for k, x in ((0, 1), (1, e)):
        gx[k] = gt[:, pl.ds(x * lane, lane)]
    pl.semaphore_wait(barrier, count)
    up_start(0)
    flat_start(0)
    up_start(1)

    def ring(a):
        for k, z in ((0, e - 1), (1, 0)):
            for side in range(2):
                rs[k, a, side, pl.ds(0, e + 2)] = lx[a, side].astype(jnp.float32)[:, z]
                rs[k, a, 2 + side, pl.ds(0, e)] = ly[a, side].astype(jnp.float32)[:, z]

    zidx = lax.broadcasted_iota(jnp.int32, (1, e, 1), 1)

    def slide(mid, lo, hi):
        below = jnp.where(zidx == 0, lo[:, None, :], pltpu.roll(mid, 1, 1))
        above = jnp.where(zidx == e - 1, hi[:, None, :], pltpu.roll(mid, e - 1, 1))
        return below.astype(pad.dtype), above.astype(pad.dtype)

    def shift(a):
        def body(x, carry):
            mid = pad[a, 1, x + 1, pl.ds(1, e)].astype(jnp.float32)
            below, above = slide(mid, zr[0, a, x], zr[1, a, x])
            pad[a, 0, x + 1, pl.ds(1, e)] = below
            pad[a, 2, x + 1, pl.ds(1, e)] = above
            return carry

        lax.fori_loop(0, e, body, 0)

    def lay(a):
        for side, at in ((0, 0), (1, e + 1)):
            pad[a, 1, at] = lx[a, side]
            pad[a, 1, pl.ds(1, e), at] = ly[a, side]

    def fill(a):
        for side, at in ((0, 0), (1, e + 1)):
            mid = lx[a, side]
            below, above = slide(
                mid.astype(jnp.float32), rr[0, a, side, pl.ds(0, e + 2)], rr[1, a, side, pl.ds(0, e + 2)]
            )
            for oz, v in ((0, below), (2, above)):
                pad[a, oz, at] = v
            mid = ly[a, side]
            below, above = slide(
                mid.astype(jnp.float32), rr[0, a, 2 + side, pl.ds(0, e)], rr[1, a, 2 + side, pl.ds(0, e)]
            )
            for oz, v in ((0, below), (2, above)):
                pad[a, oz, pl.ds(1, e), at] = v

    def rows(a, oz, x0, nx):
        v = pad[a, oz, pl.ds(x0, nx)].reshape(nx, half + 1, 2, e, ch)
        parts = [
            v[:, i // 2:i // 2 + half, i % 2].reshape(nx * half * e, ch) for i in range(4)
        ]
        return jnp.concatenate(parts, axis=1)

    def terms(oz, carry):
        acc = jnp.zeros((6 * ch, 4 * ch), jnp.float32)
        for x in range(0, e, PAIR):
            left = jnp.concatenate(
                [gt[:, (x + 2 - ox) * lane:(x + 2 - ox + PAIR) * lane] for ox in range(3)], axis=0
            )
            acc = acc + jnp.dot(left, rows(0, oz, x + 1, PAIR), preferred_element_type=jnp.float32)
        for ox in range(3):
            top = 2 * ox * ch
            for oy in range(3):
                block = (
                    acc[top:top + ch, oy * ch:(oy + 1) * ch]
                    + acc[top + ch:top + 2 * ch, (oy + 1) * ch:(oy + 2) * ch]
                )
                src[pl.ds((ox * 9 + oy * 3 + oz) * tap, tap)] = block.reshape(tap, TILE, ch)
        return carry

    def border(oz, first, last):
        ends = [pad[0, oz, pl.ds(1, e), y].reshape(e * e, ch) for y in (0, e + 1)]
        by_y = jnp.dot(
            gy[first * 2 * ch:last * 2 * ch], jnp.concatenate(ends, axis=1),
            preferred_element_type=jnp.float32,
        )
        for ox in range(first, last):
            if ox != 1:
                x = ox // 2 * (e + 1)
                by_x = jnp.dot(
                    gx[ox // 2], rows(0, oz, x, 1), preferred_element_type=jnp.float32
                )
            for oy in range(3):
                at = pl.ds((ox * 9 + oy * 3 + oz) * tap, tap)
                block = src[at].reshape(ch, ch)
                if oy != 1:
                    top, side = (2 * (ox - first) + oy // 2) * ch, oy // 2 * ch
                    block = block + by_y[top:top + ch, side:side + ch]
                if ox != 1:
                    block = block + by_x[:ch, oy * ch:(oy + 1) * ch]
                    block = block + by_x[ch:, (oy + 1) * ch:(oy + 2) * ch]
                src[at] = block.T.reshape(tap, TILE, ch)

    def to_mate(source, target, send, recv, mate):
        return pltpu.make_async_remote_copy(
            src_ref=source, dst_ref=target, send_sem=send, recv_sem=recv,
            device_id=mate, device_id_type=MESH,
        )

    def parts(s):
        base, size = groups[s]
        return base, size // 2, size // 2 // blk

    def core_copy(s):
        base, half_size, _ = parts(s)
        return to_mate(
            src.at[pl.ds(base + (1 - core_bit) * half_size, half_size)],
            land.at[pl.ds(base // 2, half_size)], csend.at[s], crecv.at[s], core,
        )

    def block_copy(s, r):
        size = pl.ds(0, parts(s)[2] + 1)
        return to_mate(
            qs.at[s, r, size], ql.at[s, r, size], rsend.at[s, r], rrecv.at[s, r], peers[r][1]
        )

    def far_copy(s, k):
        size = pl.ds(0, parts(s)[2] + 1)
        return to_mate(fs.at[s, k, size], fl.at[s, k, size], fsend.at[s, k], frecv.at[s, k], far[k][1])

    def gather_copy(s, r):
        size = pl.ds(0, parts(s)[2] + 1)
        return to_mate(
            aq.at[s, 0, size], aq.at[s, r, size], gsend.at[s, r], grecv.at[s, r], peers[r][1]
        )

    def back_copy(s, r):
        size = pl.ds(0, parts(s)[2] + 1)
        return to_mate(aq.at[s, r, size], cq.at[s, r, size], bsend.at[s, r], brecv.at[s, r], core)

    near_first = sorted(range(1, blk), key=lambda r: bin(r).count("1"))

    def encode(v):
        top = jnp.max(jnp.abs(v), axis=0)
        power = jnp.clip(jnp.ceil(jnp.log2(top)), -126.0, 126.0)
        code = jnp.round(v * jnp.exp2(-power) * LEVELS)
        return code.astype(jnp.int32).astype(jnp.int16), power.astype(jnp.int32).astype(jnp.int16)

    def decode(code, power):
        scale = jnp.exp2(power.astype(jnp.int32).astype(jnp.float32))
        return code.astype(jnp.int32).astype(jnp.float32) * (1.0 / LEVELS) * scale

    def put_code(ref, size, v):
        code, power = encode(v)
        ref[pl.ds(0, size)] = code
        ref[size] = power

    def get_code(ref, size):
        return decode(ref[pl.ds(0, size)], ref[size])

    def begin(s):
        core_copy(s).start()

    def split(s):
        base, half_size, size = parts(s)
        core_copy(s).wait()
        order = sorted(range(1, blk), key=lambda r: -bin(r).count("1")) + [0]
        for r in order:
            at = peers[r][0] * size
            v = src[pl.ds(base + core_bit * half_size + at, size)] + land[pl.ds(base // 2 + at, size)]
            if r == 0:
                own[s, pl.ds(0, size)] = v
            else:
                put_code(qs.at[s, r], size, v)
                block_copy(s, r).start()

    def spread_out(s, v):
        put_code(aq.at[s, 0], parts(s)[2], v * factor)
        for r in sorted(range(1, blk), key=lambda r: -bin(r).count("1")):
            gather_copy(s, r).start()
        back_copy(s, 0).start()

    def join(s):
        size = parts(s)[2]
        v = own[s, pl.ds(0, size)]
        for r in range(1, blk):
            block_copy(s, r).wait()
            v = v + get_code(ql.at[s, r], size)
        if far:
            put_code(fs.at[s, 0], size, v)
            far_copy(s, 0).start()
        else:
            spread_out(s, v)

    def cross(s, k):
        size = parts(s)[2]
        far_copy(s, k).wait()
        mine, theirs = fs[s, k, pl.ds(0, size + 1)].astype(jnp.int32), fl[s, k, pl.ds(0, size + 1)].astype(jnp.int32)
        low = jnp.where(far[k][0] == 0, mine, theirs)
        high = jnp.where(far[k][0] == 0, theirs, mine)
        v = decode(low[:size], low[size]) + decode(high[:size], high[size])
        if k + 1 < len(far):
            put_code(fs.at[s, k + 1], size, v)
            far_copy(s, k + 1).start()
        else:
            spread_out(s, v)

    def unpack(s, ref, bit, r):
        base, half_size, size = parts(s)
        dw_ref[pl.ds(base + bit * half_size + peers[r][0] * size, size)] = get_code(ref.at[s, r], size)

    def relay(s):
        unpack(s, aq, core_bit, 0)
        for r in near_first:
            gather_copy(s, r).wait()
            back_copy(s, r).start()
            unpack(s, aq, core_bit, r)

    def close(s):
        for r in [0] + near_first:
            back_copy(s, r).wait()
            unpack(s, cq, 1 - core_bit, r)

    nx = 4

    def conv(a, c):
        x0 = c * nx
        acc = jnp.zeros((nx * half * e, 2 * ch), jnp.float32)
        for t in range(9):
            acc = acc + jnp.dot(
                rows(a, t % 3, x0 + t // 3, nx), wx[a, t], preferred_element_type=jnp.float32
            )
        for p in range(2):
            obuf[a, pl.ds(x0, nx), :, p] = (
                acc[:, p * ch:(p + 1) * ch].reshape(nx, half, 2, BE, ch).astype(obuf.dtype)
            )

    def put(a, dst):
        for s in range(8):
            p = pos_ref[0, s]
            v = obuf[
                a, pl.ds(p // 4 * BE, BE), pl.ds(lax.rem(p // 2, 2) * (BE // 2), BE // 2), :,
                lax.rem(p, 2),
            ].reshape(BE, BE, BE, ch)
            dst[s] = jnp.where(s < cnt_ref[0, 0], v, jnp.zeros_like(v))

    def circle():
        flat_finish(1)
        ring(1)
        ring_start(1)

    def ready():
        lay(1)
        ring_finish(1)
        fill(1)
        up_finish(1)
        shift(1)

    work = []
    for a, dst in ((0, out_ref), (1, dx_ref)):
        if a == 1:
            work.append(ready)
        for c in range(e // nx):
            work.append(functools.partial(conv, a, c))
        if a == 0:
            work.append(circle)
        work.append(functools.partial(put, a, dst))

    terms(1, 0)
    up_finish(0)
    shift(0)
    used = 27 * tap
    if src.shape[0] > used:
        src[pl.ds(used, src.shape[0] - used)] = jnp.zeros((src.shape[0] - used, TILE, ch), src.dtype)
    lax.fori_loop(0, 2, lambda i, carry: terms(2 * i, carry), 0)
    flat_finish(0)
    flat_start(1)
    ring(0)
    ring_start(0)
    lay(0)
    border(1, 0, 2)
    ring_finish(0)
    fill(0)
    border(0, 0, 2)
    border(2, 0, 2)
    begin(0)
    for oz in range(3):
        border(oz, 2, 3)
    begin(1)
    lax.fori_loop(0, 9, spread, 0)

    def do(n):
        for _ in range(n):
            if work:
                work.pop(0)()

    def meet(s):
        for k in range(len(far)):
            cross(s, k)

    split(0)
    split(1)
    do(5)
    join(0)
    do(2)
    join(1)
    do(1)
    meet(0)
    do(1)
    meet(1)
    do(len(work))
    relay(0)
    close(0)
    relay(1)
    close(1)


def leave(rows, *refs):
    sources, targets, sem = refs[:3], refs[3:6], refs[6]
    copies = [
        pltpu.make_async_copy(
            source.at[pl.ds(0, rows)] if k == 2 else source, target, sem.at[k]
        )
        for k, (source, target) in enumerate(zip(sources, targets))
    ]
    for copy in copies[::-1]:
        copy.start()
    for copy in copies:
        copy.wait()


def fused(features, cotangent, weight, pos, cnt, factor, n_tomo, n_brick):
    slots, vox, ch = features.shape
    e = 2 * BE
    half = e // 2
    n = n_tomo * n_brick
    tb, bb = n_tomo.bit_length() - 1, n_brick.bit_length() - 1
    blk = 1 << (tb + 1)
    unit = 2 * blk
    units = -(-weight.shape[0] * (ch // TILE) // unit)
    first = units // 2
    groups = [(0, first * unit), (first * unit, (units - first) * unit)]
    total = units * unit
    piece = (units - first) + 1
    far = max(bb - 2, 1)
    vm = pl.BlockSpec(memory_space=pltpu.VMEM)
    hbm = pl.BlockSpec(memory_space=pl.ANY)
    brick = jax.ShapeDtypeStruct((slots, BE, BE, BE, ch), jnp.bfloat16)
    dma = pltpu.SemaphoreType.DMA
    taps = weight.shape[0] * ch // TILE
    results = pl.pallas_call(
        functools.partial(kernel, factor, tb, bb, groups),
        out_shape=(
            pltpu.VMEM(brick.shape, jnp.bfloat16), pltpu.VMEM(brick.shape, jnp.bfloat16),
            pltpu.VMEM((total, TILE, ch), jnp.float32),
        ),
        in_specs=[pl.BlockSpec(memory_space=pltpu.HBM)] * 5,
        out_specs=(vm, vm, vm),
        scratch_shapes=[
            pltpu.SMEM(pos.shape, jnp.int32), pltpu.SMEM(cnt.shape, jnp.int32),
            pltpu.VMEM(brick.shape, jnp.bfloat16), pltpu.VMEM(brick.shape, jnp.bfloat16),
            pltpu.VMEM(weight.shape, jnp.bfloat16),
            pltpu.VMEM((2, 3, e + 2, e + 2, e, ch), jnp.bfloat16),
            pltpu.VMEM((2, 2, e, e, ch), jnp.float32),
            pltpu.VMEM((2, 2, e, e, ch), jnp.float32),
            pltpu.VMEM((2, 2, e + 2, e, ch), jnp.bfloat16),
            pltpu.VMEM((2, 2, e, e, ch), jnp.bfloat16),
            pltpu.VMEM((2, 2, 4, e + 8, ch), jnp.float32),
            pltpu.VMEM((2, 2, 4, e + 8, ch), jnp.float32),
            pltpu.VMEM((2, 9, 4 * ch, 2 * ch), jnp.bfloat16),
            pltpu.VMEM((2 * ch, (e + 2) * half * e), jnp.bfloat16),
            pltpu.VMEM((6 * ch, e * e), jnp.bfloat16),
            pltpu.VMEM((2, 2 * ch, half * e), jnp.bfloat16),
            pltpu.VMEM((2, e, half, 2, 2, BE, ch), jnp.bfloat16),
            pltpu.VMEM((total, TILE, ch), jnp.float32),
            pltpu.VMEM((total // 2, TILE, ch), jnp.float32),
            pltpu.VMEM((2, piece - 1, TILE, ch), jnp.float32),
            pltpu.VMEM((2, blk, piece, TILE, ch), jnp.int16),
            pltpu.VMEM((2, blk, piece, TILE, ch), jnp.int16),
            pltpu.VMEM((2, far, piece, TILE, ch), jnp.int16),
            pltpu.VMEM((2, far, piece, TILE, ch), jnp.int16),
            pltpu.VMEM((2, blk, piece, TILE, ch), jnp.int16),
            pltpu.VMEM((2, blk, piece, TILE, ch), jnp.int16),
            dma((5,)), dma((2, 2)), dma((2, 2)), dma((2, 8)), dma((2, 8)),
            dma((2, 2)), dma((2, 2)), dma((2,)), dma((2,)), dma((2, blk)), dma((2, blk)),
            dma((2, blk)), dma((2, blk)), dma((2, far)), dma((2, far)), dma((2, blk)), dma((2, blk)),
        ],
        compiler_params=pltpu.CompilerParams(
            collective_id=0, has_side_effects=True, vmem_limit_bytes=59 << 20
        ),
        name="fused",
    )(
        pos, cnt,
        features.reshape(slots, BE, BE, BE, ch), cotangent.reshape(slots, BE, BE, BE, ch), weight,
    )
    out, dx, dw = pl.pallas_call(
        functools.partial(leave, taps),
        out_shape=(brick, brick, jax.ShapeDtypeStruct((taps, TILE, ch), jnp.float32)),
        in_specs=[hbm] * 3,
        out_specs=(hbm,) * 3,
        scratch_shapes=[dma((3,))],
        compiler_params=pltpu.CompilerParams(vmem_limit_bytes=1 << 20),
        name="leave",
    )(*results)
    return out, dx, dw.reshape(weight.shape)


def shards(features, weight, cotangent, brick_pos, brick_count):
    slots, vox, ch = features.shape[1:]
    n_tomo, n_brick = lax.axis_size("tomo"), lax.axis_size("brick")
    factor = 1.0 / math.sqrt(n_tomo * n_brick * slots * vox)
    out, dx, dw = fused(
        features[0], cotangent[0], weight, brick_pos, brick_count, factor, n_tomo, n_brick
    )
    return out.reshape(1, slots, vox, ch), dx.reshape(1, slots, vox, ch), dw


def solution(mesh):
    in_specs = (
        P("tomo", "brick", None, None),
        P(),
        P("tomo", "brick", None, None),
        P("tomo", "brick"),
        P("tomo", "brick"),
    )
    out_specs = (P("tomo", "brick", None, None), P("tomo", "brick", None, None), P())
    return jax.shard_map(shards, mesh=mesh, in_specs=in_specs, out_specs=out_specs, check_vma=False)
```

```python
import functools
import math

import jax
import jax.numpy as jnp
from jax import lax
from jax.experimental import pallas as pl
from jax.experimental.pallas import tpu as pltpu
from jax.sharding import PartitionSpec as P

BE = 8
MESH = pl.DeviceIdType.MESH
TILE = 16
LEVELS = 32000.0
PAIR = 2


def coords_of(index, levels):
    out = []
    for bit in (2, 1, 0):
        c = 0
        for level in range(levels):
            c = c + lax.rem(index // (1 << (3 * level + bit)), 2) * (1 << level)
        out.append(c)
    return out


def index_of(coords, levels):
    i = 0
    for bit, c in zip((2, 1, 0), coords):
        for level in range(levels):
            i = i + lax.rem(c // (1 << level), 2) * (1 << (3 * level + bit))
    return i


def kernel(
    factor, tb, bb, groups,
    pos_hbm, cnt_hbm, f_hbm, g_hbm, w_hbm,
    out_ref, dx_ref, dw_ref,
    pos_ref, cnt_ref, f_ref, g_ref, w_ref, pad, zs, zr, lx, ly, rs, rr, wx, gt, gy, gx, obuf, src, land, own, qs, ql, fs, fl, aq, cq,
    isem, hsend, hrecv, psend, precv, esend, erecv, csend, crecv, bsend, brecv, rsend, rrecv, fsend, frecv, gsend, grecv,
):
    e = 2 * BE
    half = e // 2
    lane = half * e
    ch = f_ref.shape[-1]
    tap = ch // TILE
    levels = bb // 3
    side = 1 << levels
    tomo = lax.axis_index("tomo")
    brick = lax.axis_index("brick")
    here = coords_of(brick, levels)

    loads = [
        pltpu.make_async_copy(source, target, isem.at[k])
        for k, (source, target) in enumerate((
            (pos_hbm, pos_ref), (cnt_hbm, cnt_ref), (f_hbm, f_ref), (g_hbm, g_ref), (w_hbm, w_ref)
        ))
    ]
    for load in loads:
        load.start()

    def neighbour(step):
        at, has = [], True
        for c, d in zip(here, step):
            at.append(lax.rem(c + d + side, side))
            if d:
                has = jnp.logical_and(has, c < side - 1 if d > 0 else c > 0)
        return has, (tomo, index_of(at, levels))

    flat = [(i, j, 0) for i in (-1, 0, 1) for j in (-1, 0, 1) if i or j]
    upright = [(0, 0, 1), (0, 0, -1)]
    near = {step: neighbour(step) for step in flat + upright}

    def mate_on(v, width):
        bit = lax.rem(v // width, 2)
        return bit, v + width - 2 * width * bit

    core_bit, core_mate = mate_on(brick, 1)
    core = (tomo, core_mate)
    flips = [(0, 1 << k) for k in range(tb)] + [(1, 2)]
    blk = 1 << len(flips)
    home = 0
    for k, (axis, width) in enumerate(flips):
        home = home + lax.rem((tomo, brick)[axis] // width, 2) * (1 << k)
    peers = []
    for r in range(blk):
        at, rank = [tomo, brick], home
        for k, (axis, width) in enumerate(flips):
            if r >> k & 1:
                at[axis] = mate_on(at[axis], width)[1]
                rank = mate_on(rank, 1 << k)[1]
        peers.append((rank, tuple(at)))
    far = []
    for k in range(2, bb):
        bit, mate = mate_on(brick, 1 << k)
        far.append((bit, (tomo, mate)))

    barrier = pltpu.get_barrier_semaphore()
    greet = [core] + [mate for _, mate in peers[1:]] + [mate for _, mate in far]
    count = len(greet)
    for mate in greet:
        pl.semaphore_signal(barrier, inc=1, device_id=mate, device_id_type=MESH)
    for has, mate in near.values():

        @pl.when(has)
        def _(mate=mate):
            pl.semaphore_signal(barrier, inc=1, device_id=mate, device_id_type=MESH)

        count = count + has.astype(jnp.int32)

    loads[0].wait()
    loads[1].wait()

    slots = []
    for p in range(8):
        s = jnp.int32(0)
        for k in range(8):
            s = jnp.where(pos_ref[0, k] == p, k, s)
        slots.append(s)

    def gather(a, ref):
        def body(x, carry):
            for q in range(4):
                parts = []
                for pz in range(2):
                    s = slots[2 * q + pz]
                    v = ref[s, x].astype(jnp.float32)
                    parts.append(jnp.where(s < cnt_ref[0, 0], v, 0.0))
                v = jnp.concatenate(parts, axis=1)
                at, y = q // 2 * BE + x, q % 2 * BE
                pad[a, 1, 1 + at, pl.ds(1 + y, BE)] = v.astype(pad.dtype)
                zs[0, a, at, pl.ds(y, BE)] = v[:, e - 1]
                zs[1, a, at, pl.ds(y, BE)] = v[:, 0]
            return carry

        lax.fori_loop(0, BE, body, 0)

    def inner(d):
        return pl.ds(1, e) if d == 0 else e if d > 0 else 1

    def landing(a, step):
        if step[0] == 0:
            return ly, (a, 0 if step[1] > 0 else 1)
        side = 0 if step[0] > 0 else 1
        return lx, (a, side, pl.ds(1, e) if step[1] == 0 else 0 if step[1] > 0 else e + 1)

    def flat_copy(a, k):
        step = flat[k]
        ref, at = landing(a, step)
        return pltpu.make_async_remote_copy(
            src_ref=pad.at[a, 1, inner(step[0]), inner(step[1])], dst_ref=ref.at[at],
            send_sem=psend.at[a, k], recv_sem=precv.at[a, k],
            device_id=near[step][1], device_id_type=MESH,
        )

    def ring_copy(a, k):
        return pltpu.make_async_remote_copy(
            src_ref=rs.at[k, a], dst_ref=rr.at[k, a],
            send_sem=esend.at[a, k], recv_sem=erecv.at[a, k],
            device_id=near[upright[k]][1], device_id_type=MESH,
        )

    def upright_copy(a, k):
        return pltpu.make_async_remote_copy(
            src_ref=zs.at[k, a], dst_ref=zr.at[k, a],
            send_sem=hsend.at[a, k], recv_sem=hrecv.at[a, k],
            device_id=near[upright[k]][1], device_id_type=MESH,
        )

    def halo_start(steps, copy, a):
        for k, step in enumerate(steps):

            @pl.when(near[step][0])
            def _(k=k):
                copy(a, k).start()

    def halo_finish(steps, copy, clear, a):
        for k, step in enumerate(steps):
            has = near[tuple(-d for d in step)][0]

            @pl.when(has)
            def _(k=k):
                copy(a, k).wait_recv()

            @pl.when(jnp.logical_not(has))
            def _(k=k):
                clear(a, k)

            @pl.when(near[step][0])
            def _(k=k):
                copy(a, k).wait_send()

    def flat_clear(a, k):
        ref, at = landing(a, flat[k])
        shape = tuple(e for d in flat[k][:2] if d == 0) + (e, ch)
        ref[at] = jnp.zeros(shape, ref.dtype)

    def up_clear(a, k):
        zr[k, a] = jnp.zeros((e, e, ch), zr.dtype)

    def ring_clear(a, k):
        rr[k, a] = jnp.zeros(rr.shape[2:], rr.dtype)

    flat_start = functools.partial(halo_start, flat, flat_copy)
    flat_finish = functools.partial(halo_finish, flat, flat_copy, flat_clear)
    up_start = functools.partial(halo_start, upright, upright_copy)
    up_finish = functools.partial(halo_finish, upright, upright_copy, up_clear)
    ring_start = functools.partial(halo_start, upright, ring_copy)
    ring_finish = functools.partial(halo_finish, upright, ring_copy, ring_clear)

    loads[2].wait()
    gather(0, f_ref)
    loads[3].wait()
    gather(1, g_ref)
    loads[4].wait()

    zero = jnp.zeros((ch, ch), wx.dtype)

    def spread(t, carry):
        ox, oz = t // 3, lax.rem(t, 3)
        for i in range(4):
            for p in range(2):
                oy = i - p
                at = (pl.ds(i * ch, ch), pl.ds(p * ch, ch))
                if 0 <= oy <= 2:
                    wx[(0, t) + at] = w_ref[ox * 9 + oy * 3 + oz]
                    wx[(1, t) + at] = w_ref[(2 - ox) * 9 + (2 - oy) * 3 + 2 - oz].T
                else:
                    wx[(0, t) + at] = zero
                    wx[(1, t) + at] = zero
        return carry

    def turn(x, carry):
        v = pad[1, 1, x + 1, pl.ds(1, e)].reshape(half, 2, e, ch)
        at = pl.ds(pl.multiple_of((x + 1) * lane, lane), lane)
        for p in range(2):
            gt[pl.ds(p * ch, ch), at] = v[:, p].reshape(lane, ch).T
        return carry

    def empty(oz, carry):
        for x in (0, e + 1):
            pad[0, oz, x] = jnp.zeros((e + 2, e, ch), pad.dtype)
        for y in (0, e + 1):
            pad[0, oz, pl.ds(1, e), y] = jnp.zeros((e, e, ch), pad.dtype)
        return carry

    lax.fori_loop(0, 3, empty, 0)
    lax.fori_loop(0, e, turn, 0)
    blank = jnp.zeros((2 * ch, lane), gt.dtype)
    gt[:, pl.ds(0, lane)] = blank
    gt[:, pl.ds((e + 1) * lane, lane)] = blank
    nil = jnp.zeros((1, e, ch), pad.dtype)
    for p, y in ((0, 1), (1, e)):
        v = pad[1, 1, pl.ds(1, e), y]
        for ox, kept in enumerate((
            jnp.concatenate([v[1:], nil], axis=0), v, jnp.concatenate([nil, v[:e - 1]], axis=0)
        )):
            gy[pl.ds((2 * ox + p) * ch, ch)] = kept.reshape(e * e, ch).T
    for k, x in ((0, 1), (1, e)):
        gx[k] = gt[:, pl.ds(x * lane, lane)]
    pl.semaphore_wait(barrier, count)
    up_start(0)
    flat_start(0)
    up_start(1)

    def ring(a):
        for k, z in ((0, e - 1), (1, 0)):
            for side in range(2):
                rs[k, a, side, pl.ds(0, e + 2)] = lx[a, side].astype(jnp.float32)[:, z]
                rs[k, a, 2 + side, pl.ds(0, e)] = ly[a, side].astype(jnp.float32)[:, z]

    zidx = lax.broadcasted_iota(jnp.int32, (1, e, 1), 1)

    def slide(mid, lo, hi):
        below = jnp.where(zidx == 0, lo[:, None, :], pltpu.roll(mid, 1, 1))
        above = jnp.where(zidx == e - 1, hi[:, None, :], pltpu.roll(mid, e - 1, 1))
        return below.astype(pad.dtype), above.astype(pad.dtype)

    def shift(a):
        def body(x, carry):
            mid = pad[a, 1, x + 1, pl.ds(1, e)].astype(jnp.float32)
            below, above = slide(mid, zr[0, a, x], zr[1, a, x])
            pad[a, 0, x + 1, pl.ds(1, e)] = below
            pad[a, 2, x + 1, pl.ds(1, e)] = above
            return carry

        lax.fori_loop(0, e, body, 0)

    def lay(a):
        for side, at in ((0, 0), (1, e + 1)):
            pad[a, 1, at] = lx[a, side]
            pad[a, 1, pl.ds(1, e), at] = ly[a, side]

    def fill(a):
        for side, at in ((0, 0), (1, e + 1)):
            mid = lx[a, side]
            below, above = slide(
                mid.astype(jnp.float32), rr[0, a, side, pl.ds(0, e + 2)], rr[1, a, side, pl.ds(0, e + 2)]
            )
            for oz, v in ((0, below), (2, above)):
                pad[a, oz, at] = v
            mid = ly[a, side]
            below, above = slide(
                mid.astype(jnp.float32), rr[0, a, 2 + side, pl.ds(0, e)], rr[1, a, 2 + side, pl.ds(0, e)]
            )
            for oz, v in ((0, below), (2, above)):
                pad[a, oz, pl.ds(1, e), at] = v

    def rows(a, oz, x0, nx):
        v = pad[a, oz, pl.ds(x0, nx)].reshape(nx, half + 1, 2, e, ch)
        parts = [
            v[:, i // 2:i // 2 + half, i % 2].reshape(nx * half * e, ch) for i in range(4)
        ]
        return jnp.concatenate(parts, axis=1)

    def terms(oz, carry):
        acc = jnp.zeros((6 * ch, 4 * ch), jnp.float32)
        for x in range(0, e, PAIR):
            left = jnp.concatenate(
                [gt[:, (x + 2 - ox) * lane:(x + 2 - ox + PAIR) * lane] for ox in range(3)], axis=0
            )
            acc = acc + jnp.dot(left, rows(0, oz, x + 1, PAIR), preferred_element_type=jnp.float32)
        for ox in range(3):
            top = 2 * ox * ch
            for oy in range(3):
                block = (
                    acc[top:top + ch, oy * ch:(oy + 1) * ch]
                    + acc[top + ch:top + 2 * ch, (oy + 1) * ch:(oy + 2) * ch]
                )
                src[pl.ds((ox * 9 + oy * 3 + oz) * tap, tap)] = block.reshape(tap, TILE, ch)
        return carry

    def border(oz, first, last):
        ends = [pad[0, oz, pl.ds(1, e), y].reshape(e * e, ch) for y in (0, e + 1)]
        by_y = jnp.dot(
            gy[first * 2 * ch:last * 2 * ch], jnp.concatenate(ends, axis=1),
            preferred_element_type=jnp.float32,
        )
        for ox in range(first, last):
            if ox != 1:
                x = ox // 2 * (e + 1)
                by_x = jnp.dot(
                    gx[ox // 2], rows(0, oz, x, 1), preferred_element_type=jnp.float32
                )
            for oy in range(3):
                at = pl.ds((ox * 9 + oy * 3 + oz) * tap, tap)
                block = src[at].reshape(ch, ch)
                if oy != 1:
                    top, side = (2 * (ox - first) + oy // 2) * ch, oy // 2 * ch
                    block = block + by_y[top:top + ch, side:side + ch]
                if ox != 1:
                    block = block + by_x[:ch, oy * ch:(oy + 1) * ch]
                    block = block + by_x[ch:, (oy + 1) * ch:(oy + 2) * ch]
                src[at] = block.T.reshape(tap, TILE, ch)

    def to_mate(source, target, send, recv, mate):
        return pltpu.make_async_remote_copy(
            src_ref=source, dst_ref=target, send_sem=send, recv_sem=recv,
            device_id=mate, device_id_type=MESH,
        )

    def parts(s):
        base, size = groups[s]
        return base, size // 2, size // 2 // blk

    def core_copy(s):
        base, half_size, _ = parts(s)
        return to_mate(
            src.at[pl.ds(base + (1 - core_bit) * half_size, half_size)],
            land.at[pl.ds(base // 2, half_size)], csend.at[s], crecv.at[s], core,
        )

    def block_copy(s, r):
        size = pl.ds(0, parts(s)[2] + 1)
        return to_mate(
            qs.at[s, r, size], ql.at[s, r, size], rsend.at[s, r], rrecv.at[s, r], peers[r][1]
        )

    def far_copy(s, k):
        size = pl.ds(0, parts(s)[2] + 1)
        return to_mate(fs.at[s, k, size], fl.at[s, k, size], fsend.at[s, k], frecv.at[s, k], far[k][1])

    def gather_copy(s, r):
        size = pl.ds(0, parts(s)[2] + 1)
        return to_mate(
            aq.at[s, 0, size], aq.at[s, r, size], gsend.at[s, r], grecv.at[s, r], peers[r][1]
        )

    def back_copy(s, r):
        size = pl.ds(0, parts(s)[2] + 1)
        return to_mate(aq.at[s, r, size], cq.at[s, r, size], bsend.at[s, r], brecv.at[s, r], core)

    near_first = sorted(range(1, blk), key=lambda r: bin(r).count("1"))

    def encode(v):
        top = jnp.max(jnp.abs(v), axis=0)
        power = jnp.clip(jnp.ceil(jnp.log2(top)), -126.0, 126.0)
        code = jnp.round(v * jnp.exp2(-power) * LEVELS)
        return code.astype(jnp.int32).astype(jnp.int16), power.astype(jnp.int32).astype(jnp.int16)

    def decode(code, power):
        scale = jnp.exp2(power.astype(jnp.int32).astype(jnp.float32))
        return code.astype(jnp.int32).astype(jnp.float32) * (1.0 / LEVELS) * scale

    def put_code(ref, size, v):
        code, power = encode(v)
        ref[pl.ds(0, size)] = code
        ref[size] = power

    def get_code(ref, size):
        return decode(ref[pl.ds(0, size)], ref[size])

    def begin(s):
        core_copy(s).start()

    def split(s):
        base, half_size, size = parts(s)
        core_copy(s).wait()
        order = sorted(range(1, blk), key=lambda r: -bin(r).count("1")) + [0]
        for r in order:
            at = peers[r][0] * size
            v = src[pl.ds(base + core_bit * half_size + at, size)] + land[pl.ds(base // 2 + at, size)]
            if r == 0:
                own[s, pl.ds(0, size)] = v
            else:
                put_code(qs.at[s, r], size, v)
                block_copy(s, r).start()

    def spread_out(s, v):
        put_code(aq.at[s, 0], parts(s)[2], v * factor)
        for r in sorted(range(1, blk), key=lambda r: -bin(r).count("1")):
            gather_copy(s, r).start()
        back_copy(s, 0).start()

    def join(s):
        size = parts(s)[2]
        v = own[s, pl.ds(0, size)]
        for r in range(1, blk):
            block_copy(s, r).wait()
            v = v + get_code(ql.at[s, r], size)
        if far:
            put_code(fs.at[s, 0], size, v)
            far_copy(s, 0).start()
        else:
            spread_out(s, v)

    def cross(s, k):
        size = parts(s)[2]
        far_copy(s, k).wait()
        mine, theirs = fs[s, k, pl.ds(0, size + 1)].astype(jnp.int32), fl[s, k, pl.ds(0, size + 1)].astype(jnp.int32)
        low = jnp.where(far[k][0] == 0, mine, theirs)
        high = jnp.where(far[k][0] == 0, theirs, mine)
        v = decode(low[:size], low[size]) + decode(high[:size], high[size])
        if k + 1 < len(far):
            put_code(fs.at[s, k + 1], size, v)
            far_copy(s, k + 1).start()
        else:
            spread_out(s, v)

    def unpack(s, ref, bit, r):
        base, half_size, size = parts(s)
        dw_ref[pl.ds(base + bit * half_size + peers[r][0] * size, size)] = get_code(ref.at[s, r], size)

    def relay(s):
        unpack(s, aq, core_bit, 0)
        for r in near_first:
            gather_copy(s, r).wait()
            back_copy(s, r).start()
            unpack(s, aq, core_bit, r)

    def close(s):
        for r in [0] + near_first:
            back_copy(s, r).wait()
            unpack(s, cq, 1 - core_bit, r)

    def conv(a, c, nx):
        x0 = c * nx
        acc = jnp.zeros((nx * half * e, 2 * ch), jnp.float32)
        for t in range(9):
            acc = acc + jnp.dot(
                rows(a, t % 3, x0 + t // 3, nx), wx[a, t], preferred_element_type=jnp.float32
            )
        for p in range(2):
            obuf[a, pl.ds(x0, nx), :, p] = (
                acc[:, p * ch:(p + 1) * ch].reshape(nx, half, 2, BE, ch).astype(obuf.dtype)
            )

    def put(a, dst):
        for s in range(8):
            p = pos_ref[0, s]
            v = obuf[
                a, pl.ds(p // 4 * BE, BE), pl.ds(lax.rem(p // 2, 2) * (BE // 2), BE // 2), :,
                lax.rem(p, 2),
            ].reshape(BE, BE, BE, ch)
            dst[s] = jnp.where(s < cnt_ref[0, 0], v, jnp.zeros_like(v))

    def circle():
        flat_finish(1)
        ring(1)
        ring_start(1)

    def ready():
        lay(1)
        ring_finish(1)
        fill(1)
        up_finish(1)
        shift(1)

    work = []
    for a, dst in ((0, out_ref), (1, dx_ref)):
        if a == 1:
            work.append(ready)
        nx = (8, 4)[a]
        for c in range(e // nx):
            work.append(functools.partial(conv, a, c, nx))
        if a == 0:
            work.append(circle)
        work.append(functools.partial(put, a, dst))

    terms(1, 0)
    up_finish(0)
    shift(0)
    used = 27 * tap
    if src.shape[0] > used:
        src[pl.ds(used, src.shape[0] - used)] = jnp.zeros((src.shape[0] - used, TILE, ch), src.dtype)
    lax.fori_loop(0, 2, lambda i, carry: terms(2 * i, carry), 0)
    flat_finish(0)
    flat_start(1)
    ring(0)
    ring_start(0)
    lay(0)
    border(1, 0, 2)
    ring_finish(0)
    fill(0)
    border(0, 0, 2)
    border(2, 0, 2)
    begin(0)
    for oz in range(3):
        border(oz, 2, 3)
    begin(1)
    lax.fori_loop(0, 9, spread, 0)

    def do(n):
        for _ in range(n):
            if work:
                work.pop(0)()

    def meet(s):
        for k in range(len(far)):
            cross(s, k)

    split(0)
    split(1)
    do(3)
    join(0)
    do(2)
    join(1)
    do(1)
    meet(0)
    do(1)
    meet(1)
    do(len(work))
    relay(0)
    relay(1)
    close(0)
    close(1)


def leave(rows, *refs):
    sources, targets, sem = refs[:3], refs[3:6], refs[6]
    copies = [
        pltpu.make_async_copy(
            source.at[pl.ds(0, rows)] if k == 2 else source, target, sem.at[k]
        )
        for k, (source, target) in enumerate(zip(sources, targets))
    ]
    for copy in copies[::-1]:
        copy.start()
    for copy in copies:
        copy.wait()


def fused(features, cotangent, weight, pos, cnt, factor, n_tomo, n_brick):
    slots, vox, ch = features.shape
    e = 2 * BE
    half = e // 2
    n = n_tomo * n_brick
    tb, bb = n_tomo.bit_length() - 1, n_brick.bit_length() - 1
    blk = 1 << (tb + 1)
    unit = 2 * blk
    units = -(-weight.shape[0] * (ch // TILE) // unit)
    first = units // 2
    groups = [(0, first * unit), (first * unit, (units - first) * unit)]
    total = units * unit
    piece = (units - first) + 1
    far = max(bb - 2, 1)
    vm = pl.BlockSpec(memory_space=pltpu.VMEM)
    hbm = pl.BlockSpec(memory_space=pl.ANY)
    brick = jax.ShapeDtypeStruct((slots, BE, BE, BE, ch), jnp.bfloat16)
    dma = pltpu.SemaphoreType.DMA
    taps = weight.shape[0] * ch // TILE
    results = pl.pallas_call(
        functools.partial(kernel, factor, tb, bb, groups),
        out_shape=(
            pltpu.VMEM(brick.shape, jnp.bfloat16), pltpu.VMEM(brick.shape, jnp.bfloat16),
            pltpu.VMEM((total, TILE, ch), jnp.float32),
        ),
        in_specs=[pl.BlockSpec(memory_space=pltpu.HBM)] * 5,
        out_specs=(vm, vm, vm),
        scratch_shapes=[
            pltpu.SMEM(pos.shape, jnp.int32), pltpu.SMEM(cnt.shape, jnp.int32),
            pltpu.VMEM(brick.shape, jnp.bfloat16), pltpu.VMEM(brick.shape, jnp.bfloat16),
            pltpu.VMEM(weight.shape, jnp.bfloat16),
            pltpu.VMEM((2, 3, e + 2, e + 2, e, ch), jnp.bfloat16),
            pltpu.VMEM((2, 2, e, e, ch), jnp.float32),
            pltpu.VMEM((2, 2, e, e, ch), jnp.float32),
            pltpu.VMEM((2, 2, e + 2, e, ch), jnp.bfloat16),
            pltpu.VMEM((2, 2, e, e, ch), jnp.bfloat16),
            pltpu.VMEM((2, 2, 4, e + 8, ch), jnp.float32),
            pltpu.VMEM((2, 2, 4, e + 8, ch), jnp.float32),
            pltpu.VMEM((2, 9, 4 * ch, 2 * ch), jnp.bfloat16),
            pltpu.VMEM((2 * ch, (e + 2) * half * e), jnp.bfloat16),
            pltpu.VMEM((6 * ch, e * e), jnp.bfloat16),
            pltpu.VMEM((2, 2 * ch, half * e), jnp.bfloat16),
            pltpu.VMEM((2, e, half, 2, 2, BE, ch), jnp.bfloat16),
            pltpu.VMEM((total, TILE, ch), jnp.float32),
            pltpu.VMEM((total // 2, TILE, ch), jnp.float32),
            pltpu.VMEM((2, piece - 1, TILE, ch), jnp.float32),
            pltpu.VMEM((2, blk, piece, TILE, ch), jnp.int16),
            pltpu.VMEM((2, blk, piece, TILE, ch), jnp.int16),
            pltpu.VMEM((2, far, piece, TILE, ch), jnp.int16),
            pltpu.VMEM((2, far, piece, TILE, ch), jnp.int16),
            pltpu.VMEM((2, blk, piece, TILE, ch), jnp.int16),
            pltpu.VMEM((2, blk, piece, TILE, ch), jnp.int16),
            dma((5,)), dma((2, 2)), dma((2, 2)), dma((2, 8)), dma((2, 8)),
            dma((2, 2)), dma((2, 2)), dma((2,)), dma((2,)), dma((2, blk)), dma((2, blk)),
            dma((2, blk)), dma((2, blk)), dma((2, far)), dma((2, far)), dma((2, blk)), dma((2, blk)),
        ],
        compiler_params=pltpu.CompilerParams(
            collective_id=0, has_side_effects=True, vmem_limit_bytes=59 << 20
        ),
        name="fused",
    )(
        pos, cnt,
        features.reshape(slots, BE, BE, BE, ch), cotangent.reshape(slots, BE, BE, BE, ch), weight,
    )
    out, dx, dw = pl.pallas_call(
        functools.partial(leave, taps),
        out_shape=(brick, brick, jax.ShapeDtypeStruct((taps, TILE, ch), jnp.float32)),
        in_specs=[hbm] * 3,
        out_specs=(hbm,) * 3,
        scratch_shapes=[dma((3,))],
        compiler_params=pltpu.CompilerParams(vmem_limit_bytes=1 << 20),
        name="leave",
    )(*results)
    return out, dx, dw.reshape(weight.shape)


def shards(features, weight, cotangent, brick_pos, brick_count):
    slots, vox, ch = features.shape[1:]
    n_tomo, n_brick = lax.axis_size("tomo"), lax.axis_size("brick")
    factor = 1.0 / math.sqrt(n_tomo * n_brick * slots * vox)
    out, dx, dw = fused(
        features[0], cotangent[0], weight, brick_pos, brick_count, factor, n_tomo, n_brick
    )
    return out.reshape(1, slots, vox, ch), dx.reshape(1, slots, vox, ch), dw


def solution(mesh):
    in_specs = (
        P("tomo", "brick", None, None),
        P(),
        P("tomo", "brick", None, None),
        P("tomo", "brick"),
        P("tomo", "brick"),
    )
    out_specs = (P("tomo", "brick", None, None), P("tomo", "brick", None, None), P())
    return jax.shard_map(shards, mesh=mesh, in_specs=in_specs, out_specs=out_specs, check_vma=False)
```
